256 devices in a mesh: sec: 64 (over y, z, core), reg: 4 (over x).
Axes of the slice: x: 4, y: 4, z: 8, core: 2. Of those that a mesh axis runs over, the one named last changes fastest.
Arguments:
- start_params: float32 [64, 4, 20, 128], P('sec', 'reg'), may hold values from -3 to 3
- right_side: float32 [64, 4, 20, 128], P('sec', 'reg'), may hold values from -40 to 40
- prior: float32 [64, 4, 20, 128], P('sec', 'reg'), may hold values from 0.1 to 1
- matches: bfloat16 [64, 4, 640, 4, 256], P('sec', 'reg'), may hold values from -1 to 1
- pair_first: int32 [64, 4, 640], P('sec', 'reg'), may hold values from 0 to 127, as said below
- pair_second: int32 [64, 4, 640], P('sec', 'reg'), may hold values from 0 to 415, as said below
- match_counts: int32 [64, 4, 640], P('sec', 'reg'), may hold values from 0 to 256, as said below
- send_lists: int32 [64, 4, 2, 16], P('sec', 'reg'), may hold values from 0 to 127, as said below
Outputs:
- solution: float32 [64, 4, 20, 128], P('sec', 'reg')
- residual: float32 [64, 4, 20, 128], P('sec', 'reg')
The draws below stay inside these ranges and needn't reach their ends.
Inputs may be any that keep to these rules, and one draw needn't show every extreme that they name: Each tile is pair_first of exactly five pairs of its device, in a drawn order. `pair_second`: names a column of the extended field; blocks of neighbours outside the grid are never named; a pair with match count 0 names its own tile. `match_counts`: 0 marks an absent pair; every device has a pair with exactly 256 matches. `send_lists`: row 0 holds the tiles whose coefficients a region lends to the region below it, row 1 to the region above; each row has 16 distinct tiles and the rows are disjoint.
All inputs are finite; a program needn't handle non-finite values.
Results may differ from the reference program's by a relative error of at most 0.0003.
Values sent between devices are 32-bit elements; how exact they have to be, the bound alone decides.
A program may use at most 64 MiB of HBM per device.

```python
import math
import jax
import jax.numpy as jnp
from jax import lax

ROWS = 16
COLS = 8
MATCHES = 256
COEFS = 20
ITERS = 1
TILE_DEV = 128
PAIR_DEV = 640
SEC_DEVS = 64
REG_DEVS = 4


def layout(key):
    devices_all = SEC_DEVS * REG_DEVS
    perm_keys = jax.random.split(jax.random.fold_in(key, 101), devices_all)
    perms = jax.vmap(lambda single: jax.random.permutation(single, TILE_DEV))(perm_keys)
    perms = perms.reshape(SEC_DEVS, REG_DEVS, TILE_DEV).astype(jnp.int32)
    order_keys = jax.random.split(jax.random.fold_in(key, 202), devices_all)
    orders = jax.vmap(lambda single: jax.random.permutation(single, PAIR_DEV))(order_keys)
    orders = orders.reshape(SEC_DEVS, REG_DEVS, PAIR_DEV).astype(jnp.int32)
    position = jnp.arange(TILE_DEV, dtype=jnp.int32)
    row_of = position // COLS
    col_of = position % COLS
    sec_of = jnp.arange(SEC_DEVS, dtype=jnp.int32)[:, None, None]
    reg_of = jnp.arange(REG_DEVS, dtype=jnp.int32)[None, :, None]
    shape_three = (SEC_DEVS, REG_DEVS, TILE_DEV)

    def local_at(target):
        index = jnp.broadcast_to(jnp.clip(target, 0, TILE_DEV - 1), shape_three)
        return jnp.take_along_axis(perms, index, axis=2)
    base = 3 * TILE_DEV
    right_live = (col_of < COLS - 1) | (reg_of < REG_DEVS - 1)
    right_second = jnp.where(col_of < COLS - 1, local_at(position + 1), base + ROWS + row_of)
    down_live = (row_of < ROWS - 1) & (reg_of >= 0)
    down_second = local_at(position + COLS)
    slant_live = (row_of < ROWS - 1) & ((col_of > 0) | (reg_of > 0))
    slant_second = jnp.where(col_of > 0, local_at(position + COLS - 1), base + row_of + 1)
    near_live = (sec_of >= 1) & (reg_of >= 0) & (position >= 0)
    near_second = TILE_DEV + jnp.roll(perms, 1, axis=0)
    far_live = (sec_of >= 2) & (reg_of >= 0) & (position >= 0)
    far_second = 2 * TILE_DEV + jnp.roll(perms, 2, axis=0)

    def joined(members):
        spread_out = [jnp.broadcast_to(member, shape_three) for member in members]
        return jnp.stack(spread_out, axis=2).reshape(SEC_DEVS, REG_DEVS, PAIR_DEV)
    live = joined([right_live, down_live, slant_live, near_live, far_live])
    seconds = joined([right_second, down_second, slant_second, near_second, far_second]).astype(jnp.int32)
    firsts = joined([perms, perms, perms, perms, perms]).astype(jnp.int32)
    counts = jax.random.randint(jax.random.fold_in(key, 303), (SEC_DEVS, REG_DEVS, PAIR_DEV), 1 + MATCHES // 8, MATCHES + 1, dtype=jnp.int32)
    counts = counts.at[:, :, 0].set(MATCHES)
    counts = jnp.where(live, counts, 0).astype(jnp.int32)
    seconds = jnp.where(live, seconds, firsts).astype(jnp.int32)

    def reorder(values):
        return jnp.take_along_axis(values, orders, axis=2)
    lists = jnp.stack([perms[:, :, ::COLS], perms[:, :, COLS - 1::COLS]], axis=2).astype(jnp.int32)
    return (reorder(firsts), reorder(seconds), reorder(counts), lists)


def draw_pair_first(key, part):
    return layout(key)[0]


def draw_pair_second(key, part):
    return layout(key)[1]


def draw_match_counts(key, part):
    return layout(key)[2]


def draw_send_lists(key, part):
    return layout(key)[3]


def draw_right_side(key, part):
    shape_four = (SEC_DEVS, REG_DEVS, COEFS, TILE_DEV)
    rising = 1.0 + 2.0 * jnp.arange(SEC_DEVS, dtype=jnp.float32)[:, None, None, None] / (SEC_DEVS - 1)
    spread_log = jax.random.uniform(jax.random.fold_in(key, 1), (SEC_DEVS, REG_DEVS, 1, TILE_DEV), minval=-1.15, maxval=1.15)
    values = jax.random.normal(jax.random.fold_in(key, 2), shape_four)
    values = jnp.clip(values, -4.0, 4.0)
    return (values * rising * jnp.exp(spread_log)).astype(jnp.float32)


def block_scale(own_key, shape, shards, smallest, largest):
    factor_of, own = 1.0, jax.random.fold_in(own_key, 6)
    for dim, shards_of in shards:
        steps = jnp.exp(jax.random.uniform(jax.random.fold_in(own, dim), (shards_of,), jnp.float32, smallest / len(shards), largest / len(shards)))
        factor_of = factor_of * jnp.repeat(steps, shape[dim] // shards_of).reshape([-1 if axis == dim else 1 for axis in range(len(shape))])
    return factor_of


def normal_values(rng, shape, deviation, bound, cuts=(), held_as=jnp.bfloat16):
    drawn = deviation * jax.random.normal(rng, shape, jnp.float32)
    if cuts:
        drawn = drawn * block_scale(rng, shape, cuts, -0.22, 0.18)
    return jnp.clip(drawn, -bound, bound).astype(held_as)


def setup_inputs(seed: int = 0) -> dict:
    seeds = jax.random.split(jax.random.key(seed), 9)
    return {
        "start_params": normal_values(seeds[0], (SEC_DEVS, REG_DEVS, COEFS, TILE_DEV), 0.5, 3.0, ((0, 64), (1, 4)), jnp.float32),
        "right_side": draw_right_side(jax.random.fold_in(seeds[8], 71), 0),
        "prior": jnp.clip(jnp.exp(math.log(1.0) - 2.3025851 * jax.random.uniform(seeds[2], (SEC_DEVS, REG_DEVS, COEFS, TILE_DEV), jnp.float32) ** block_scale(seeds[2], (SEC_DEVS, REG_DEVS, COEFS, TILE_DEV), ((0, 64), (1, 4)), -0.2, 0.2)), 0.1, 1.0),
        "matches": jnp.clip(jax.random.uniform(seeds[3], (SEC_DEVS, REG_DEVS, PAIR_DEV, 4, MATCHES), jnp.float32, -1.0, 1.0) * block_scale(seeds[3], (SEC_DEVS, REG_DEVS, PAIR_DEV, 4, MATCHES), ((0, 64), (1, 4)), -0.4, 0.0), -1.0, 1.0).astype(jnp.bfloat16),
        "pair_first": draw_pair_first(jax.random.fold_in(seeds[8], 71), 0),
        "pair_second": draw_pair_second(jax.random.fold_in(seeds[8], 71), 0),
        "match_counts": draw_match_counts(jax.random.fold_in(seeds[8], 71), 0),
        "send_lists": draw_send_lists(jax.random.fold_in(seeds[8], 71), 0),
    }


def monomials(across, upward):
    constant = jnp.ones_like(across)
    square_a = across * across
    square_b = upward * upward
    mixed = across * upward
    return jnp.stack([constant, across, upward, square_a, mixed, square_b,
                      square_a * across, square_a * upward, square_b * across, square_b * upward])


def block_terms(extended, first_blk, second_blk, count_blk, match_blk):
    points = match_blk.astype(jnp.float32)
    width = first_blk.shape[0]
    slots = points.shape[-1]
    basis_a = monomials(points[:, 0], points[:, 1])
    basis_b = monomials(points[:, 2], points[:, 3])
    weights = jnp.where(jnp.arange(slots)[None, :] < count_blk[:, None], 2.0 / slots, 0.0).astype(jnp.float32)
    own = jnp.take(extended, first_blk, axis=1).reshape(2, 10, width)
    other = jnp.take(extended, second_blk, axis=1).reshape(2, 10, width)
    high = lax.Precision.HIGHEST
    mismatch = (jnp.einsum('mpk,cmp->cpk', basis_a, own, precision=high)
                - jnp.einsum('mpk,cmp->cpk', basis_b, other, precision=high)) * weights[None]
    to_own = jnp.einsum('mpk,cpk->cmp', basis_a, mismatch, precision=high).reshape(20, width)
    to_other = -jnp.einsum('mpk,cpk->cmp', basis_b, mismatch, precision=high).reshape(20, width)
    return to_own, to_other


def device_terms(extended, first, second, counts, matches):
    pairs = first.shape[0]
    block = math.gcd(pairs, 512)
    blocks = pairs // block
    slots = matches.shape[-1]

    def one_block(items):
        return block_terms(extended, items[0], items[1], items[2], items[3])

    to_own, to_other = lax.map(one_block, (first.reshape(blocks, block), second.reshape(blocks, block),
                                           counts.reshape(blocks, block), matches.reshape(blocks, block, 4, slots)))
    to_own = jnp.moveaxis(to_own, 0, 1).reshape(20, pairs)
    to_other = jnp.moveaxis(to_other, 0, 1).reshape(20, pairs)
    total = jnp.zeros((20, extended.shape[1]), jnp.float32)
    return total.at[:, first].add(to_own).at[:, second].add(to_other)


def apply_normal(params, prior, matches, pair_first, pair_second, match_counts, send_lists):
    sections, regions = params.shape[0], params.shape[1]
    tiles = params.shape[3]
    rows = send_lists.shape[3]
    near = jnp.concatenate([jnp.zeros_like(params[:1]), params[:-1]], 0)
    far = jnp.concatenate([jnp.zeros_like(params[:2]), params[:-2]], 0)
    pick = jax.vmap(jax.vmap(lambda field, index: jnp.take(field, index, axis=1)))
    down_list = pick(params, send_lists[:, :, 0])
    up_list = pick(params, send_lists[:, :, 1])
    from_lower = jnp.concatenate([jnp.zeros_like(up_list[:, :1]), up_list[:, :-1]], 1)
    from_upper = jnp.concatenate([down_list[:, 1:], jnp.zeros_like(down_list[:, :1])], 1)
    extended = jnp.concatenate([params, near, far, from_lower, from_upper], 3)
    flat = sections * regions

    def per_device(items):
        return device_terms(items[0], items[1], items[2], items[3], items[4])

    terms = lax.map(per_device, (extended.reshape((flat,) + extended.shape[2:]),
                                 pair_first.reshape(flat, -1), pair_second.reshape(flat, -1),
                                 match_counts.reshape(flat, -1), matches.reshape((flat,) + matches.shape[2:])))
    terms = terms.reshape((sections, regions) + terms.shape[1:])
    local = terms[..., :tiles]
    near_part = terms[..., tiles:2 * tiles]
    far_part = terms[..., 2 * tiles:3 * tiles]
    local = local + jnp.concatenate([near_part[1:], jnp.zeros_like(near_part[:1])], 0)
    local = local + jnp.concatenate([far_part[2:], jnp.zeros_like(far_part[:2])], 0)
    lower_part = terms[..., 3 * tiles:3 * tiles + rows]
    upper_part = terms[..., 3 * tiles + rows:]
    to_down = jnp.concatenate([jnp.zeros_like(upper_part[:, :1]), upper_part[:, :-1]], 1)
    to_up = jnp.concatenate([lower_part[:, 1:], jnp.zeros_like(lower_part[:, :1])], 1)
    add_at = jax.vmap(jax.vmap(lambda field, index, extra: field.at[:, index].add(extra)))
    local = add_at(local, send_lists[:, :, 0], to_down)
    local = add_at(local, send_lists[:, :, 1], to_up)
    return local + prior * params


def reference(start_params, right_side, prior, matches, pair_first, pair_second, match_counts, send_lists):
    def normal(field):
        return apply_normal(field, prior, matches, pair_first, pair_second, match_counts, send_lists)

    solution = start_params
    residual = right_side - normal(start_params)
    direction = residual
    norm_now = jnp.sum(residual * residual)
    for iteration in range(ITERS):
        image = normal(direction)
        alpha = norm_now / jnp.sum(direction * image)
        solution = solution + alpha * direction
        residual = residual - alpha * image
        if iteration + 1 < ITERS:
            norm_next = jnp.sum(residual * residual)
            direction = residual + (norm_next / norm_now) * direction
            norm_now = norm_next
    return solution, residual
```

```python
import functools

import jax
import jax.numpy as jnp
from jax import lax
from jax.experimental import pallas as pl
from jax.experimental.pallas import tpu as pltpu
from jax.sharding import PartitionSpec as P

F32, BF16 = jnp.float32, jnp.bfloat16
MESH = pl.DeviceIdType.MESH
EXPONENTS = [(0, 0), (1, 0), (0, 1), (2, 0), (1, 1), (0, 2), (3, 0), (2, 1), (1, 2), (0, 3)]
MOMENTS = [(i, d - i) for d in range(1, 7) for i in range(d, -1, -1)]
TILES = 128
LANES = 128
FIELD = 32
UNROLL = 8


def powers(x, y):
    x2, xy, y2 = x * x, x * y, y * y
    return [None, x, y, x2, xy, y2, x2 * x, x2 * y, y2 * x, y2 * y]


def moments(x, y):
    base = dict(zip(EXPONENTS, powers(x, y)))
    known = dict(base)
    for i, j in MOMENTS:
        if (i, j) not in known:
            a = next(e for e in EXPONENTS[:2:-1] if (i - e[0], j - e[1]) in base)
            known[i, j] = base[a] * base[i - a[0], j - a[1]]
    return [known[e] for e in MOMENTS]


def row_of(n):
    return 16 * (n // 10) + n % 10


def gram_tile(coords, gram, tile, count, slots):
    zero = jnp.zeros((8, LANES), F32)
    gram[tile, :, 8:16, :] = jnp.zeros((20, 8, LANES), F32)
    gram[tile, :, 24:32, :] = jnp.zeros((20, 8, LANES), F32)

    def sums(terms, which):
        def step(i, totals):
            for u in range(UNROLL):
                at = pl.multiple_of((i * UNROLL + u) * 8, 8)
                new = terms(*[coords[c, pl.ds(at, 8), :] for c in which])
                totals = tuple(a + b for a, b in zip(totals, new))
            return totals

        totals = lax.fori_loop(0, slots // 8 // UNROLL, step, (zero,) * 27)
        return [jnp.sum(t, axis=0, keepdims=True) for t in totals]

    def put(n, m, row):
        r = row_of(m)
        gram[tile, n, r : r + 1, :] = row

    for side in range(2):
        table = dict(zip(MOMENTS, sums(moments, (2 * side, 2 * side + 1))))
        table[0, 0] = count
        for n, (i, j) in enumerate(EXPONENTS):
            for m, (k, l) in enumerate(EXPONENTS):
                put(10 * side + n, 10 * side + m, table[i + k, j + l])
        for n, e in enumerate(EXPONENTS):
            if side == 1:
                put(0, 10 + n, table[e])
                put(10 + n, 0, table[e])
            elif n:
                put(10, n, table[e])
                put(n, 10, table[e])
    for group in range(3):
        some = range(1 + 3 * group, 4 + 3 * group)

        def terms(xa, ya, xb, yb):
            a, b = powers(xa, ya), powers(xb, yb)
            return [a[m] * b[n] for m in some for n in range(1, 10)]

        rows = iter(sums(terms, (0, 1, 2, 3)))
        for m in some:
            for n in range(1, 10):
                row = next(rows)
                put(m, 10 + n, row)
                put(10 + n, m, row)


def thirds(x):
    high = x.astype(BF16)
    rest = x - high.astype(F32)
    middle = rest.astype(BF16)
    low = (rest - middle.astype(F32)).astype(BF16)
    return jnp.concatenate([high, middle, low], axis=0)


def joined(x):
    rows = x.shape[0] // 3
    return x[:rows] + x[rows : 2 * rows] + x[2 * rows :]


def matmul(a, b):
    return lax.dot_general(a, b, (((1,), (0,)), ((), ())), preferred_element_type=F32)


def matmul_t(a, b):
    return lax.dot_general(a, b, (((1,), (1,)), ((), ())), preferred_element_type=F32)


def kernel(
    sizes, params_hbm, side_hbm, prior_hbm, matches_hbm, first_ref, second_ref, count_ref, lists_ref,
    solution_ref, residual_ref,
    params, side, prior, points, coords, gram, own_hot, other_hot, z_ref,
    direction, lists_in, halo_in, fold_out, fold_in, part, part_in,
    load_sem, field_sem, list_send, list_recv, halo_send, halo_recv, fold_send, fold_recv, part_send, part_recv,
):
    secs, regs, group = sizes
    sec, reg = lax.axis_index("sec"), lax.axis_index("reg")
    pairs = first_ref.shape[1]
    slots = matches_hbm.shape[2]
    chunks = pairs // LANES
    rows = secs // group
    part_count = rows * regs

    def device(by_sec, by_reg):
        return (lax.rem(sec + by_sec + secs, secs), lax.rem(reg + by_reg + regs, regs))

    borrowers = [device(1, 0), device(2, 0), device(0, 1), device(0, -1)]
    owners = [device(-1, 0), device(-2, 0), device(0, -1), device(0, 1)]
    base, place = group * (sec // group), lax.rem(sec, group)
    line = [(base + lax.rem(place + j, group), reg) for j in range(1, group)]
    here = (sec // group) * regs + reg
    plane = []
    for j in range(1, part_count):
        there = lax.rem(here + j, part_count)
        plane.append(((there // regs) * group + place, lax.rem(there, regs)))

    barrier = pltpu.get_barrier_semaphore()
    for peer in borrowers + owners[:2] + line + plane:
        pl.semaphore_signal(barrier, inc=1, device_id=peer, device_id_type=MESH)

    loads = []
    for i in range(chunks):
        loads.append(pltpu.make_async_copy(matches_hbm.at[pl.ds(i * LANES, LANES)], points.at[i], load_sem.at[i]))
    fields = []
    for i, (source, target) in enumerate(((params_hbm, params), (side_hbm, side), (prior_hbm, prior))):
        for c in range(2):
            fields.append(
                pltpu.make_async_copy(
                    source.at[pl.ds(10 * c, 10), 0, :], target.at[pl.ds(16 * c, 10), :], field_sem.at[2 * i + c]
                )
            )
    for target in (params, side, prior):
        for c in range(2):
            target[16 * c + 8 : 16 * c + 16, :] = jnp.zeros((8, TILES), F32)
    for copy in fields + loads:
        copy.start()

    def send(source, target, send_sem, recv_sem, peer):
        copy = pltpu.make_async_remote_copy(
            src_ref=source, dst_ref=target, send_sem=send_sem, recv_sem=recv_sem, device_id=peer, device_id_type=MESH
        )
        copy.start()
        return copy

    def send_halo(source, turn):
        return [
            send(source, halo_in.at[turn, i], halo_send.at[turn, i], halo_recv.at[turn, i], borrowers[i])
            for i in range(4)
        ]

    def send_fold(turn):
        return [
            send(fold_out.at[turn, i], fold_in.at[turn, i], fold_send.at[turn, i], fold_recv.at[turn, i], owners[i])
            for i in range(4)
        ]

    for copy in fields:
        copy.wait()
    pl.semaphore_wait(barrier, 6 + len(line) + len(plane))
    halo = send_halo(params, 0)
    borders = [
        send(lists_ref, lists_in.at[0], list_send.at[0], list_recv.at[0], borrowers[2]),
        send(lists_ref, lists_in.at[1], list_send.at[1], list_recv.at[1], borrowers[3]),
    ]

    r = lax.broadcasted_iota(jnp.int32, (4 * LANES, 4 * LANES), 0)
    s = lax.broadcasted_iota(jnp.int32, (4 * LANES, 4 * LANES), 1)
    sort = jnp.where(r == 4 * lax.rem(s, LANES) + s // LANES, 1.0, 0.0).astype(BF16)
    slot = lax.broadcasted_iota(jnp.int32, (slots, LANES), 0)
    for copy in loads:
        copy.wait()

    @pl.loop(0, chunks)
    def _(tile):
        count = count_ref[tile]
        turned = lax.dot_general(
            points[tile].reshape(4 * LANES, slots), sort, (((0,), (0,)), ((), ())), preferred_element_type=F32
        )
        live = slot < count
        for c in range(4):
            coords[c] = jnp.where(live, turned[:, c * LANES : (c + 1) * LANES], 0.0)
        gram_tile(coords, gram, tile, count.astype(F32), slots)

    for copy in borders:
        copy.wait()
    second = second_ref[...]
    width = lists_ref.shape[1]
    index = jnp.where(second < 3 * TILES, second, -1).astype(F32)
    for i in range(2):
        start = 3 * TILES + i * width
        spot = lax.broadcasted_iota(jnp.int32, (width, pairs), 0) + start
        named = jnp.where(spot == second, 1.0, 0.0).astype(BF16)
        tile_at = matmul((lists_in[i] + 1).astype(F32).astype(BF16), named)[1 - i : 2 - i]
        index = jnp.where(tile_at > 0, tile_at + float((3 + i) * TILES - 1), index)
    index = index.astype(jnp.int32)
    column = lax.broadcasted_iota(jnp.int32, (TILES, pairs), 0)
    own_hot[...] = jnp.where(column == first_ref[...], 1.0, 0.0).astype(BF16)
    for i in range(5):
        other_hot[i * TILES : (i + 1) * TILES, :] = jnp.where(column + i * TILES == index, -1.0, 0.0).astype(BF16)

    def gathered(field, turn, halo):
        mine = thirds(field)
        own = joined(matmul(mine, own_hot[...]))
        other = matmul(mine, other_hot[:TILES, :])
        for copy in halo:
            copy.wait()
        others = jnp.concatenate([thirds(halo_in[turn, i]) for i in range(4)], axis=1)
        other = joined(other + matmul(others, other_hot[TILES:, :]))
        z_ref[0] = own
        z_ref[1] = other

    scale = 2.0 / slots

    def products():
        own, other = ([], []), ([], [])
        for tile in range(chunks):
            at = slice(tile * LANES, (tile + 1) * LANES)
            totals = [None, None]
            for n in range(20):
                block = gram[tile, n]
                for c in range(2):
                    row = 16 * c + n % 10
                    term = block * z_ref[n // 10, row : row + 1, at]
                    totals[c] = term if totals[c] is None else totals[c] + term
            for c in range(2):
                own[c].append(totals[c][:16] * scale)
                other[c].append(totals[c][16:] * scale)
        return tuple(
            jnp.concatenate([jnp.concatenate(half[c], axis=1) for c in range(2)], axis=0) for half in (own, other)
        )

    def scattered(own, other, turn):
        others = thirds(other)
        lent = joined(matmul_t(others, other_hot[TILES:, :]))
        for i in range(4):
            fold_out[turn, i] = lent[:, i * TILES : (i + 1) * TILES]
        fold = send_fold(turn)
        local = joined(matmul_t(thirds(own), own_hot[...]) + matmul_t(others, other_hot[:TILES, :]))
        return fold, local

    def folded(fold, local, turn):
        for copy in fold:
            copy.wait()
        return local + fold_in[turn, 0] + fold_in[turn, 1] + fold_in[turn, 2] + fold_in[turn, 3]

    start = params[...]
    gathered(start, 0, halo)
    own, other = products()
    fold, local = scattered(own, other, 0)
    local = local + prior[...] * start
    residual = side[...] - folded(fold, local, 0)

    direction[...] = residual
    halo = send_halo(direction, 1)
    squares = jnp.sum(residual * residual, keepdims=True)
    damped = prior[...] * residual
    gathered(residual, 1, halo)
    own, other = products()
    energy = jnp.sum(own * z_ref[0] + other * z_ref[1], keepdims=True) + jnp.sum(damped * residual, keepdims=True)
    lane = lax.broadcasted_iota(jnp.int32, (1, LANES), 1)
    total = jnp.where(lane < LANES // 2, squares, energy)
    part[0, 0:1, :] = total

    def send_part(turn, peers):
        return [
            send(
                part.at[turn, pl.ds(0, 1), :], part_in.at[turn, pl.ds(j, 1), :],
                part_send.at[turn, j], part_recv.at[turn, j], peer,
            )
            for j, peer in enumerate(peers)
        ]

    sums = send_part(0, line)
    fold, local = scattered(own, other, 1)
    local = local + damped
    for copy in sums:
        copy.wait()
    total = total + jnp.sum(part_in[0, : len(line), :], axis=0, keepdims=True)
    part[1, 0:1, :] = total
    sums = send_part(1, plane)
    image = folded(fold, local, 1)
    for copy in sums:
        copy.wait()
    total = total + jnp.sum(part_in[1, : len(plane), :], axis=0, keepdims=True)
    alpha = total[:, 0:1] / total[:, LANES // 2 : LANES // 2 + 1]
    answer = start + alpha * residual
    left = residual - alpha * image
    for c in range(2):
        for value, target in ((answer, solution_ref), (left, residual_ref)):
            target[10 * c : 10 * c + 10, :] = value[16 * c : 16 * c + 10]


def on_device(sizes, start_params, right_side, prior, matches, pair_first, pair_second, match_counts, send_lists):
    pairs, slots = matches.shape[2], matches.shape[4]
    width = send_lists.shape[3]
    secs, regs, group = sizes
    part_rows = -(-max(group, secs // group * regs) // 8) * 8
    chunks = pairs // LANES
    vmem = pl.BlockSpec(memory_space=pltpu.VMEM)
    hbm = pl.BlockSpec(memory_space=pl.ANY)
    field = (FIELD, TILES)
    dma = pltpu.SemaphoreType.DMA
    answer, left = pl.pallas_call(
        functools.partial(kernel, sizes),
        out_shape=(jax.ShapeDtypeStruct((20, TILES), F32),) * 2,
        in_specs=[hbm, hbm, hbm, hbm, vmem, vmem, vmem, vmem],
        out_specs=(vmem, vmem),
        scratch_shapes=[
            pltpu.VMEM(field, F32),
            pltpu.VMEM(field, F32),
            pltpu.VMEM(field, F32),
            pltpu.VMEM((chunks, LANES, 4, slots), BF16),
            pltpu.VMEM((4, slots, LANES), F32),
            pltpu.VMEM((chunks, 20, FIELD, LANES), F32),
            pltpu.VMEM((TILES, pairs), BF16),
            pltpu.VMEM((5 * TILES, pairs), BF16),
            pltpu.VMEM((2, FIELD, pairs), F32),
            pltpu.VMEM(field, F32),
            pltpu.VMEM((2, 2, width), jnp.int32),
            pltpu.VMEM((2, 4, *field), F32),
            pltpu.VMEM((2, 4, *field), F32),
            pltpu.VMEM((2, 4, *field), F32),
            pltpu.VMEM((2, 8, LANES), F32),
            pltpu.VMEM((2, part_rows, LANES), F32),
            dma((chunks,)),
            dma((6,)),
            dma((2,)),
            dma((2,)),
            dma((2, 4)),
            dma((2, 4)),
            dma((2, 4)),
            dma((2, 4)),
            dma((2, part_rows)),
            dma((2, part_rows)),
        ],
        compiler_params=pltpu.CompilerParams(collective_id=0, has_side_effects=True, vmem_limit_bytes=40 * 2**20),
    )(
        start_params.reshape(20, 1, TILES),
        right_side.reshape(20, 1, TILES),
        prior.reshape(20, 1, TILES),
        matches.reshape(pairs, 4, slots),
        pair_first.reshape(1, pairs),
        pair_second.reshape(1, pairs),
        match_counts.reshape(chunks, 1, LANES),
        send_lists.reshape(2, width),
    )
    return answer[None, None], left[None, None]


def solution(mesh):
    secs, regs = mesh.shape["sec"], mesh.shape["reg"]
    group = 16 if secs % 16 == 0 else secs
    wide = P("sec", "reg", None, None)
    return jax.shard_map(
        functools.partial(on_device, (secs, regs, group)),
        mesh=mesh,
        in_specs=(
            wide, wide, wide, P("sec", "reg", None, None, None),
            P("sec", "reg", None), P("sec", "reg", None), P("sec", "reg", None), wide,
        ),
        out_specs=(wide, wide),
        check_vma=False,
    )
```

```python
import functools

import jax
import jax.numpy as jnp
from jax import lax
from jax.experimental import pallas as pl
from jax.experimental.pallas import tpu as pltpu
from jax.sharding import PartitionSpec as P

F32, BF16 = jnp.float32, jnp.bfloat16
MESH = pl.DeviceIdType.MESH
EXPONENTS = [(0, 0), (1, 0), (0, 1), (2, 0), (1, 1), (0, 2), (3, 0), (2, 1), (1, 2), (0, 3)]
MOMENTS = [(i, d - i) for d in range(1, 7) for i in range(d, -1, -1)]
TILES = 128
LANES = 128
FIELD = 32
UNROLL = 16
EARLY = 2


def powers(x, y):
    x2, xy, y2 = x * x, x * y, y * y
    return [None, x, y, x2, xy, y2, x2 * x, x2 * y, y2 * x, y2 * y]


def moments(x, y):
    base = dict(zip(EXPONENTS, powers(x, y)))
    known = dict(base)
    for i, j in MOMENTS:
        if (i, j) not in known:
            a = next(e for e in EXPONENTS[:2:-1] if (i - e[0], j - e[1]) in base)
            known[i, j] = base[a] * base[i - a[0], j - a[1]]
    return [known[e] for e in MOMENTS]


def row_of(n):
    return 16 * (n // 10) + n % 10


def gram_tile(coords, gram, tile, count, slots):
    zero = jnp.zeros((8, LANES), F32)
    gram[tile, :, 8:16, :] = jnp.zeros((20, 8, LANES), F32)
    gram[tile, :, 24:32, :] = jnp.zeros((20, 8, LANES), F32)

    def sums(terms, which):
        def step(i, totals):
            for u in range(UNROLL):
                at = pl.multiple_of((i * UNROLL + u) * 8, 8)
                new = terms(*[coords[c, pl.ds(at, 8), :] for c in which])
                totals = tuple(a + b for a, b in zip(totals, new))
            return totals

        totals = lax.fori_loop(0, slots // 8 // UNROLL, step, (zero,) * 27)
        return [jnp.sum(t, axis=0, keepdims=True) for t in totals]

    def put(n, m, row):
        r = row_of(m)
        gram[tile, n, r : r + 1, :] = row

    for side in range(2):
        table = dict(zip(MOMENTS, sums(moments, (2 * side, 2 * side + 1))))
        table[0, 0] = count
        for n, (i, j) in enumerate(EXPONENTS):
            for m, (k, l) in enumerate(EXPONENTS):
                put(10 * side + n, 10 * side + m, table[i + k, j + l])
        for n, e in enumerate(EXPONENTS):
            if side == 1:
                put(0, 10 + n, table[e])
                put(10 + n, 0, table[e])
            elif n:
                put(10, n, table[e])
                put(n, 10, table[e])
    for group in range(3):
        some = range(1 + 3 * group, 4 + 3 * group)

        def terms(xa, ya, xb, yb):
            a, b = powers(xa, ya), powers(xb, yb)
            return [a[m] * b[n] for m in some for n in range(1, 10)]

        rows = iter(sums(terms, (0, 1, 2, 3)))
        for m in some:
            for n in range(1, 10):
                row = next(rows)
                put(m, 10 + n, row)
                put(10 + n, m, row)


def thirds(x):
    high = x.astype(BF16)
    rest = x - high.astype(F32)
    middle = rest.astype(BF16)
    low = (rest - middle.astype(F32)).astype(BF16)
    return jnp.concatenate([high, middle, low], axis=0)


def joined(x):
    rows = x.shape[0] // 3
    return x[:rows] + x[rows : 2 * rows] + x[2 * rows :]


def matmul(a, b):
    return lax.dot_general(a, b, (((1,), (0,)), ((), ())), preferred_element_type=F32)


def matmul_t(a, b):
    return lax.dot_general(a, b, (((1,), (1,)), ((), ())), preferred_element_type=F32)


def kernel(
    sizes, params_hbm, side_hbm, prior_hbm, matches_hbm, first_hbm, second_hbm, count_hbm, lists_hbm,
    solution_ref, residual_ref,
    first_ref, second_ref, count_ref, lists_ref, params, side, prior, points, coords, gram, own_hot, other_hot, z_ref,
    direction, lists_in, halo_in, fold_out, fold_in, part, part_in,
    load_sem, small_sem, field_sem, list_send, list_recv, halo_send, halo_recv, fold_send, fold_recv, part_send, part_recv,
):
    secs, regs, group = sizes
    sec, reg = lax.axis_index("sec"), lax.axis_index("reg")
    pairs = first_hbm.shape[1]
    slots = matches_hbm.shape[2]
    chunks = pairs // LANES
    rows = secs // group
    part_count = rows * regs

    def device(by_sec, by_reg):
        return (lax.rem(sec + by_sec + secs, secs), lax.rem(reg + by_reg + regs, regs))

    borrowers = [device(1, 0), device(2, 0), device(0, 1), device(0, -1)]
    owners = [device(-1, 0), device(-2, 0), device(0, -1), device(0, 1)]
    base, place = group * (sec // group), lax.rem(sec, group)
    line = [(base + lax.rem(place + j, group), reg) for j in range(1, group)]
    here = (sec // group) * regs + reg
    plane = []
    for j in range(1, part_count):
        there = lax.rem(here + j, part_count)
        plane.append(((there // regs) * group + place, lax.rem(there, regs)))

    barrier = pltpu.get_barrier_semaphore()
    for peer in borrowers + owners[:2] + line + plane:
        pl.semaphore_signal(barrier, inc=1, device_id=peer, device_id_type=MESH)

    loads = []
    for i in range(chunks):
        loads.append(pltpu.make_async_copy(matches_hbm.at[pl.ds(i * LANES, LANES)], points.at[i], load_sem.at[i]))
    fields = []
    for i, (source, target) in enumerate(((params_hbm, params), (side_hbm, side), (prior_hbm, prior))):
        for c in range(2):
            fields.append(
                pltpu.make_async_copy(
                    source.at[pl.ds(10 * c, 10), 0, :], target.at[pl.ds(16 * c, 10), :], field_sem.at[2 * i + c]
                )
            )
    for target in (params, side, prior):
        for c in range(2):
            target[16 * c + 8 : 16 * c + 16, :] = jnp.zeros((8, TILES), F32)
    small = [
        pltpu.make_async_copy(source, target, small_sem.at[i])
        for i, (source, target) in enumerate(
            ((lists_hbm, lists_ref), (count_hbm, count_ref), (first_hbm, first_ref), (second_hbm, second_ref))
        )
    ]
    for copy in fields[:2] + small[:1] + loads[:1] + small[1:2] + loads[1:] + small[2:] + fields[2:]:
        copy.start()

    sent = []

    def send(source, target, send_sem, recv_sem, peer):
        copy = pltpu.make_async_remote_copy(
            src_ref=source, dst_ref=target, send_sem=send_sem, recv_sem=recv_sem, device_id=peer, device_id_type=MESH
        )
        copy.start()
        sent.append(copy)
        return copy

    def send_halo(source, turn):
        return [
            send(source, halo_in.at[turn, i], halo_send.at[turn, i], halo_recv.at[turn, i], borrowers[i])
            for i in range(4)
        ]

    def send_fold(turn):
        return [
            send(fold_out.at[turn, i], fold_in.at[turn, i], fold_send.at[turn, i], fold_recv.at[turn, i], owners[i])
            for i in range(4)
        ]

    r = lax.broadcasted_iota(jnp.int32, (4 * LANES, 4 * LANES), 0)
    s = lax.broadcasted_iota(jnp.int32, (4 * LANES, 4 * LANES), 1)
    sort = jnp.where(r == 4 * lax.rem(s, LANES) + s // LANES, 1.0, 0.0).astype(BF16)
    slot = lax.broadcasted_iota(jnp.int32, (slots, LANES), 0)

    def form(tile):
        count = count_ref[tile]
        turned = lax.dot_general(
            points[tile].reshape(4 * LANES, slots), sort, (((0,), (0,)), ((), ())), preferred_element_type=F32
        )
        live = slot < count
        for c in range(4):
            coords[c] = jnp.where(live, turned[:, c * LANES : (c + 1) * LANES], 0.0)
        gram_tile(coords, gram, tile, count.astype(F32), slots)

    for copy in small[1:] + fields[2:] + loads:
        copy.wait()
    pl.loop(0, EARLY)(form)
    for copy in fields[:2] + small[:1]:
        copy.wait()
    pl.semaphore_wait(barrier, 6 + len(line) + len(plane))
    halo = send_halo(params, 0)
    borders = [
        send(lists_ref, lists_in.at[0], list_send.at[0], list_recv.at[0], borrowers[2]),
        send(lists_ref, lists_in.at[1], list_send.at[1], list_recv.at[1], borrowers[3]),
    ]


    pl.loop(EARLY, chunks)(form)

    for copy in borders:
        copy.wait_recv()
    second = second_ref[...]
    width = lists_ref.shape[1]
    index = jnp.where(second < 3 * TILES, second, -1).astype(F32)
    for i in range(2):
        start = 3 * TILES + i * width
        spot = lax.broadcasted_iota(jnp.int32, (width, pairs), 0) + start
        named = jnp.where(spot == second, 1.0, 0.0).astype(BF16)
        tile_at = matmul((lists_in[i] + 1).astype(F32).astype(BF16), named)[1 - i : 2 - i]
        index = jnp.where(tile_at > 0, tile_at + float((3 + i) * TILES - 1), index)
    index = index.astype(jnp.int32)
    column = lax.broadcasted_iota(jnp.int32, (TILES, pairs), 0)
    own_hot[...] = jnp.where(column == first_ref[...], 1.0, 0.0).astype(BF16)
    for i in range(5):
        other_hot[i * TILES : (i + 1) * TILES, :] = jnp.where(column + i * TILES == index, -1.0, 0.0).astype(BF16)

    def gathered(field, turn, halo):
        mine = thirds(field)
        own = joined(matmul(mine, own_hot[...]))
        other = matmul(mine, other_hot[:TILES, :])
        for copy in halo:
            copy.wait_recv()
        others = jnp.concatenate([thirds(halo_in[turn, i]) for i in range(4)], axis=1)
        other = joined(other + matmul(others, other_hot[TILES:, :]))
        z_ref[0] = own
        z_ref[1] = other

    scale = 2.0 / slots

    def products():
        own, other = ([], []), ([], [])
        for tile in range(chunks):
            at = slice(tile * LANES, (tile + 1) * LANES)
            totals = [None, None]
            for n in range(20):
                block = gram[tile, n]
                for c in range(2):
                    row = 16 * c + n % 10
                    term = block * z_ref[n // 10, row : row + 1, at]
                    totals[c] = term if totals[c] is None else totals[c] + term
            for c in range(2):
                own[c].append(totals[c][:16] * scale)
                other[c].append(totals[c][16:] * scale)
        return tuple(
            jnp.concatenate([jnp.concatenate(half[c], axis=1) for c in range(2)], axis=0) for half in (own, other)
        )

    def scattered(own, other, turn):
        others = thirds(other)
        lent = joined(matmul_t(others, other_hot[TILES:, :]))
        for i in range(4):
            fold_out[turn, i] = lent[:, i * TILES : (i + 1) * TILES]
        fold = send_fold(turn)
        local = joined(matmul_t(thirds(own), own_hot[...]) + matmul_t(others, other_hot[:TILES, :]))
        return fold, local

    def folded(fold, local, turn):
        for copy in fold:
            copy.wait_recv()
        return local + fold_in[turn, 0] + fold_in[turn, 1] + fold_in[turn, 2] + fold_in[turn, 3]

    start = params[...]
    gathered(start, 0, halo)
    own, other = products()
    fold, local = scattered(own, other, 0)
    local = local + prior[...] * start
    residual = side[...] - folded(fold, local, 0)

    direction[...] = residual
    halo = send_halo(direction, 1)
    squares = jnp.sum(residual * residual, keepdims=True)
    damped = prior[...] * residual
    gathered(residual, 1, halo)
    own, other = products()
    energy = jnp.sum(own * z_ref[0] + other * z_ref[1], keepdims=True) + jnp.sum(damped * residual, keepdims=True)
    lane = lax.broadcasted_iota(jnp.int32, (1, LANES), 1)
    total = jnp.where(lane < LANES // 2, squares, energy)
    part[0, 0:1, :] = total

    def send_part(turn, peers):
        return [
            send(
                part.at[turn, pl.ds(0, 1), :], part_in.at[turn, pl.ds(j, 1), :],
                part_send.at[turn, j], part_recv.at[turn, j], peer,
            )
            for j, peer in enumerate(peers)
        ]

    sums = send_part(0, line)
    fold, local = scattered(own, other, 1)
    local = local + damped
    for copy in sums:
        copy.wait_recv()
    total = total + jnp.sum(part_in[0, : len(line), :], axis=0, keepdims=True)
    part[1, 0:1, :] = total
    sums = send_part(1, plane)
    image = folded(fold, local, 1)
    for copy in sums:
        copy.wait_recv()
    total = total + jnp.sum(part_in[1, : len(plane), :], axis=0, keepdims=True)
    alpha = total[:, 0:1] / total[:, LANES // 2 : LANES // 2 + 1]
    for copy in sent:
        copy.wait_send()
    answer = start + alpha * residual
    left = residual - alpha * image
    for c in range(2):
        for value, target in ((answer, solution_ref), (left, residual_ref)):
            target[10 * c : 10 * c + 10, :] = value[16 * c : 16 * c + 10]


def on_device(sizes, start_params, right_side, prior, matches, pair_first, pair_second, match_counts, send_lists):
    pairs, slots = matches.shape[2], matches.shape[4]
    width = send_lists.shape[3]
    secs, regs, group = sizes
    part_rows = -(-max(group, secs // group * regs) // 8) * 8
    chunks = pairs // LANES
    vmem = pl.BlockSpec(memory_space=pltpu.VMEM)
    hbm = pl.BlockSpec(memory_space=pltpu.HBM)
    field = (FIELD, TILES)
    dma = pltpu.SemaphoreType.DMA
    answer, left = pl.pallas_call(
        functools.partial(kernel, sizes),
        out_shape=(jax.ShapeDtypeStruct((20, TILES), F32),) * 2,
        in_specs=[hbm] * 8,
        out_specs=(vmem, vmem),
        scratch_shapes=[
            pltpu.VMEM((1, pairs), jnp.int32),
            pltpu.VMEM((1, pairs), jnp.int32),
            pltpu.VMEM((chunks, 1, LANES), jnp.int32),
            pltpu.VMEM((2, width), jnp.int32),
            pltpu.VMEM(field, F32),
            pltpu.VMEM(field, F32),
            pltpu.VMEM(field, F32),
            pltpu.VMEM((chunks, LANES, 4, slots), BF16),
            pltpu.VMEM((4, slots, LANES), F32),
            pltpu.VMEM((chunks, 20, FIELD, LANES), F32),
            pltpu.VMEM((TILES, pairs), BF16),
            pltpu.VMEM((5 * TILES, pairs), BF16),
            pltpu.VMEM((2, FIELD, pairs), F32),
            pltpu.VMEM(field, F32),
            pltpu.VMEM((2, 2, width), jnp.int32),
            pltpu.VMEM((2, 4, *field), F32),
            pltpu.VMEM((2, 4, *field), F32),
            pltpu.VMEM((2, 4, *field), F32),
            pltpu.VMEM((2, 8, LANES), F32),
            pltpu.VMEM((2, part_rows, LANES), F32),
            dma((chunks,)),
            dma((4,)),
            dma((6,)),
            dma((2,)),
            dma((2,)),
            dma((2, 4)),
            dma((2, 4)),
            dma((2, 4)),
            dma((2, 4)),
            dma((2, part_rows)),
            dma((2, part_rows)),
        ],
        compiler_params=pltpu.CompilerParams(collective_id=0, has_side_effects=True, vmem_limit_bytes=32 * 2**20),
    )(*[pltpu.with_memory_space_constraint(x, pltpu.HBM) for x in (
        start_params.reshape(20, 1, TILES),
        right_side.reshape(20, 1, TILES),
        prior.reshape(20, 1, TILES),
        matches.reshape(pairs, 4, slots),
        pair_first.reshape(1, pairs),
        pair_second.reshape(1, pairs),
        match_counts.reshape(chunks, 1, LANES),
        send_lists.reshape(2, width),
    )])
    return answer[None, None], left[None, None]


def solution(mesh):
    secs, regs = mesh.shape["sec"], mesh.shape["reg"]
    group = 16 if secs % 16 == 0 else secs
    wide = P("sec", "reg", None, None)
    return jax.shard_map(
        functools.partial(on_device, (secs, regs, group)),
        mesh=mesh,
        in_specs=(
            wide, wide, wide, P("sec", "reg", None, None, None),
            P("sec", "reg", None), P("sec", "reg", None), P("sec", "reg", None), wide,
        ),
        out_specs=(wide, wide),
        check_vma=False,
    )
```

```python
import functools

import jax
import jax.numpy as jnp
from jax import lax
from jax.experimental import pallas as pl
from jax.experimental.pallas import tpu as pltpu
from jax.sharding import PartitionSpec as P

F32, BF16 = jnp.float32, jnp.bfloat16
MESH = pl.DeviceIdType.MESH
EXPONENTS = [(0, 0), (1, 0), (0, 1), (2, 0), (1, 1), (0, 2), (3, 0), (2, 1), (1, 2), (0, 3)]
MOMENTS = [(i, d - i) for d in range(1, 7) for i in range(d, -1, -1)]
TILES = 128
LANES = 128
FIELD = 32
UNROLL = 16
EARLY = 1
FORMED = 3
GROUPS = ((1, 2, 3), (4, 5, 6), (7, 8, 9))


def powers(x, y):
    x2, xy, y2 = x * x, x * y, y * y
    return [None, x, y, x2, xy, y2, x2 * x, x2 * y, y2 * x, y2 * y]


def moments(x, y):
    base = dict(zip(EXPONENTS, powers(x, y)))
    known = dict(base)
    for i, j in MOMENTS:
        if (i, j) not in known:
            a = next(e for e in EXPONENTS[:2:-1] if (i - e[0], j - e[1]) in base)
            known[i, j] = base[a] * base[i - a[0], j - a[1]]
    return [known[e] for e in MOMENTS]


def row_of(n):
    return 16 * (n // 10) + n % 10


def gram_tile(coords, gram, tile, valid, slots):
    zero = jnp.zeros((8, LANES), F32)
    gram[tile, :, 8:16, :] = jnp.zeros((20, 8, LANES), F32)
    gram[tile, :, 24:32, :] = jnp.zeros((20, 8, LANES), F32)

    def sums(terms, which, count):
        def step(i, totals):
            for u in range(UNROLL):
                at = pl.multiple_of((i * UNROLL + u) * 8, 8)
                new = terms(*[coords[c, pl.ds(at, 8), :] for c in which])
                totals = tuple(a + b for a, b in zip(totals, new))
            return totals

        trips = slots // 8 // UNROLL
        totals = step(0, (zero,) * count) if trips == 1 else lax.fori_loop(0, trips, step, (zero,) * count)
        return [jnp.sum(t, axis=0, keepdims=True) for t in totals]

    def put(n, m, row):
        r = row_of(m)
        gram[tile, n, r : r + 1, :] = row

    for side in range(2):
        table = dict(zip(MOMENTS, sums(moments, (2 * side, 2 * side + 1), 27)))
        table[0, 0] = valid
        for n, (i, j) in enumerate(EXPONENTS):
            for m, (k, l) in enumerate(EXPONENTS):
                put(10 * side + n, 10 * side + m, table[i + k, j + l])
        for n, e in enumerate(EXPONENTS):
            if side == 1:
                put(0, 10 + n, table[e])
                put(10 + n, 0, table[e])
            elif n:
                put(10, n, table[e])
                put(n, 10, table[e])
    for some in GROUPS:

        def terms(xa, ya, xb, yb):
            a, b = powers(xa, ya), powers(xb, yb)
            return [a[m] * b[n] for m in some for n in range(1, 10)]

        rows = iter(sums(terms, (0, 1, 2, 3), 9 * len(some)))
        for m in some:
            for n in range(1, 10):
                row = next(rows)
                put(m, 10 + n, row)
                put(10 + n, m, row)


def thirds(x):
    high = x.astype(BF16)
    rest = x - high.astype(F32)
    middle = rest.astype(BF16)
    low = (rest - middle.astype(F32)).astype(BF16)
    return jnp.concatenate([high, middle, low], axis=0)


def joined(x):
    rows = x.shape[0] // 3
    return x[:rows] + x[rows : 2 * rows] + x[2 * rows :]


def matmul(a, b):
    return lax.dot_general(a, b, (((1,), (0,)), ((), ())), preferred_element_type=F32)


def matmul_t(a, b):
    return lax.dot_general(a, b, (((1,), (1,)), ((), ())), preferred_element_type=F32)


def kernel(
    sizes, params_hbm, side_hbm, prior_hbm, matches_hbm, first_hbm, second_hbm, count_hbm, lists_hbm,
    solution_ref, residual_ref,
    first_ref, second_ref, count_ref, lists_ref, params, side, prior, points, coords, sort_ref, gram, own_hot, other_hot, z_ref,
    y_ref, direction, lists_in, halo_in, fold_out, fold_in, part, part_in,
    load_sem, small_sem, field_sem, list_send, list_recv, halo_send, halo_recv, fold_send, fold_recv, part_send, part_recv,
):
    secs, regs, group = sizes
    sec, reg = lax.axis_index("sec"), lax.axis_index("reg")
    pairs = first_hbm.shape[1]
    slots = matches_hbm.shape[2]
    chunks = pairs // LANES
    rows = secs // group

    def device(by_sec, by_reg):
        return (lax.rem(sec + by_sec + secs, secs), lax.rem(reg + by_reg + regs, regs))

    borrowers = [device(1, 0), device(2, 0), device(0, 1), device(0, -1)]
    owners = [device(-1, 0), device(-2, 0), device(0, -1), device(0, 1)]
    base, place = group * (sec // group), lax.rem(sec, group)
    line = [(base + lax.rem(place + j, group), reg) for j in sorted(range(1, group), key=lambda j: abs(2 * j - group))]
    hops = [(min(a, rows - a) + min(b, regs - b), a, b) for a in range(rows) for b in range(regs) if a or b]
    plane = [
        (lax.rem(sec // group + a, rows) * group + place, lax.rem(reg + b, regs)) for _, a, b in sorted(hops, reverse=True)
    ]

    loads = []
    for i in range(chunks):
        loads.append(pltpu.make_async_copy(matches_hbm.at[pl.ds(i * LANES, LANES)], points.at[i], load_sem.at[i]))
    fields = []
    for i, (source, target) in enumerate(((params_hbm, params), (side_hbm, side), (prior_hbm, prior))):
        for c in range(2):
            fields.append(
                pltpu.make_async_copy(
                    source.at[pl.ds(10 * c, 10), 0, :], target.at[pl.ds(16 * c, 10), :], field_sem.at[2 * i + c]
                )
            )
    for target in (params, side, prior):
        for c in range(2):
            target[16 * c + 10 : 16 * c + 16, :] = jnp.zeros((6, TILES), F32)
    small = [
        pltpu.make_async_copy(source, target, small_sem.at[i])
        for i, (source, target) in enumerate(
            ((lists_hbm, lists_ref), (count_hbm, count_ref), (first_hbm, first_ref), (second_hbm, second_ref))
        )
    ]
    for copy in fields[:2] + small[:1] + loads[:1] + small[1:2] + loads[1:] + small[2:] + fields[2:]:
        copy.start()

    barrier = pltpu.get_barrier_semaphore()
    for peer in borrowers + owners[:2] + line + plane:
        pl.semaphore_signal(barrier, inc=1, device_id=peer, device_id_type=MESH)

    sent = []

    def send(source, target, send_sem, recv_sem, peer):
        copy = pltpu.make_async_remote_copy(
            src_ref=source, dst_ref=target, send_sem=send_sem, recv_sem=recv_sem, device_id=peer, device_id_type=MESH
        )
        copy.start()
        sent.append(copy)
        return copy

    def send_halo(source, turn):
        return [
            send(source, halo_in.at[turn, i], halo_send.at[turn, i], halo_recv.at[turn, i], borrowers[i])
            for i in range(4)
        ]

    def send_fold(turn):
        return [
            send(fold_out.at[turn, i], fold_in.at[turn, i], fold_send.at[turn, i], fold_recv.at[turn, i], owners[i])
            for i in range(4)
        ]

    r = lax.broadcasted_iota(jnp.int32, (4 * LANES, 4 * LANES), 0)
    s = lax.broadcasted_iota(jnp.int32, (4 * LANES, 4 * LANES), 1)
    sort_ref[...] = jnp.where(r == 4 * lax.rem(s, LANES) + s // LANES, 1.0, 0.0).astype(BF16)
    slot = lax.broadcasted_iota(jnp.int32, (slots, LANES), 0)

    def turn(tile, to):
        turned = lax.dot_general(
            points[tile].reshape(4 * LANES, slots), sort_ref[...], (((0,), (0,)), ((), ())), preferred_element_type=F32
        )
        live = slot < count_ref[tile]
        for c in range(4):
            coords[to, c] = jnp.where(live, turned[:, c * LANES : (c + 1) * LANES], 0.0)
        coords[to, 4] = jnp.where(live, 1.0, 0.0)

    def gram_of(tile, at):
        gram_tile(coords.at[at], gram, tile, count_ref[tile].astype(F32), slots)

    def form(tile):
        at = lax.rem(tile, 2)
        turn(tile, at)
        gram_of(tile, at)

    for copy in small[1:] + fields[2:] + loads:
        copy.wait()
    pl.loop(0, EARLY)(form)
    for copy in fields[:2] + small[:1]:
        copy.wait()
    pl.semaphore_wait(barrier, 6 + len(line) + len(plane))
    halo = send_halo(params, 0)
    borders = [
        send(lists_ref, lists_in.at[0], list_send.at[0], list_recv.at[0], borrowers[2]),
        send(lists_ref, lists_in.at[1], list_send.at[1], list_recv.at[1], borrowers[3]),
    ]


    pl.loop(EARLY, FORMED)(form)
    for tile in range(FORMED, chunks):
        turn(tile, tile % 2)

    for copy in borders:
        copy.wait_recv()
    second = second_ref[...]
    width = lists_ref.shape[1]
    index = jnp.where(second < 3 * TILES, second, -1).astype(F32)
    for i in range(2):
        start = 3 * TILES + i * width
        spot = lax.broadcasted_iota(jnp.int32, (width, pairs), 0) + start
        named = jnp.where(spot == second, 1.0, 0.0).astype(BF16)
        tile_at = matmul((lists_in[i] + 1).astype(F32).astype(BF16), named)[1 - i : 2 - i]
        index = jnp.where(tile_at > 0, tile_at + float((3 + i) * TILES - 1), index)
    index = index.astype(jnp.int32)
    column = lax.broadcasted_iota(jnp.int32, (TILES, pairs), 0)
    own_hot[...] = jnp.where(column == first_ref[...], 1.0, 0.0).astype(BF16)
    for i in range(5):
        other_hot[i * TILES : (i + 1) * TILES, :] = jnp.where(column + i * TILES == index, -1.0, 0.0).astype(BF16)

    def gathered(field, turn, halo):
        mine = thirds(field)
        own = joined(matmul(mine, own_hot[...]))
        other = matmul(mine, other_hot[:TILES, :])
        for copy in halo:
            copy.wait_recv()
        others = jnp.concatenate([thirds(halo_in[turn, i]) for i in range(4)], axis=1)
        other = joined(other + matmul(others, other_hot[TILES:, :]))
        z_ref[0] = own
        z_ref[1] = other

    scale = 2.0 / slots

    def products(tiles):
        for tile in range(tiles):
            at = slice(tile * LANES, (tile + 1) * LANES)
            totals = [None, None]
            for n in range(20):
                block = gram[tile, n]
                for c in range(2):
                    row = 16 * c + n % 10
                    term = block * z_ref[n // 10, row : row + 1, at]
                    totals[c] = term if totals[c] is None else totals[c] + term
            for c in range(2):
                for half in range(2):
                    y_ref[half, 16 * c : 16 * c + 16, at] = totals[c][16 * half : 16 * half + 16]

    def direct(tile):
        at = slice(tile * LANES, (tile + 1) * LANES)
        points_of = coords.at[tile % 2]
        for c in range(2):
            z = [[z_ref[half, 16 * c + m : 16 * c + m + 1, at] for m in range(10)] for half in range(2)]
            constant = z[0][0] + z[1][0]

            def step(i, totals):
                for u in range(UNROLL):
                    here = pl.multiple_of((i * UNROLL + u) * 8, 8)
                    xa, ya, xb, yb, live = [points_of[d, pl.ds(here, 8), :] for d in range(5)]
                    basis = powers(xa, ya)[1:] + powers(xb, yb)[1:]
                    first_half, second_half = constant + z[0][1] * xa, z[1][1] * xb
                    for m in range(1, 9):
                        first_half = first_half + z[0][m + 1] * basis[m]
                        second_half = second_half + z[1][m + 1] * basis[9 + m]
                    mismatch = (first_half + second_half) * live
                    totals = (totals[0] + mismatch,) + tuple(t + b * mismatch for t, b in zip(totals[1:], basis))
                return totals

            totals = lax.fori_loop(0, slots // 8 // UNROLL, step, (jnp.zeros((8, LANES), F32),) * 19)
            totals = [jnp.sum(t, axis=0, keepdims=True) for t in totals]
            for half in range(2):
                y_ref[half, 16 * c : 16 * c + 1, at] = totals[0]
                for m in range(1, 10):
                    y_ref[half, 16 * c + m : 16 * c + m + 1, at] = totals[9 * half + m]

    def scattered(turn):
        own, other = y_ref[0] * scale, y_ref[1] * scale
        others = thirds(other)
        lent = joined(matmul_t(others, other_hot[TILES:, :]))
        for i in range(4):
            fold_out[turn, i] = lent[:, i * TILES : (i + 1) * TILES]
        fold = send_fold(turn)
        local = joined(matmul_t(thirds(own), own_hot[...]) + matmul_t(others, other_hot[:TILES, :]))
        return fold, local

    def folded(fold, local, turn):
        for copy in fold:
            copy.wait_recv()
        return local + fold_in[turn, 0] + fold_in[turn, 1] + fold_in[turn, 2] + fold_in[turn, 3]

    start = params[...]
    gathered(start, 0, halo)
    for c in range(2):
        for half in range(2):
            y_ref[half, 16 * c + 10 : 16 * c + 16, :] = jnp.zeros((6, pairs), F32)
    for tile in range(FORMED, chunks):
        direct(tile)
    products(FORMED)
    fold, local = scattered(0)
    for tile in range(FORMED, chunks - 1):
        gram_of(tile, tile % 2)
    local = local + prior[...] * start
    residual = side[...] - folded(fold, local, 0)

    direction[...] = residual
    halo = send_halo(direction, 1)
    gram_of(chunks - 1, (chunks - 1) % 2)
    squares = jnp.sum(residual * residual, keepdims=True)
    damped = prior[...] * residual
    gathered(residual, 1, halo)
    products(chunks)
    energy = scale * jnp.sum(y_ref[0] * z_ref[0] + y_ref[1] * z_ref[1], keepdims=True) + jnp.sum(damped * residual, keepdims=True)
    lane = lax.broadcasted_iota(jnp.int32, (1, LANES), 1)
    total = jnp.where(lane < LANES // 2, squares, energy)
    part[0, 0:1, :] = total

    def send_part(turn, peers):
        return [
            send(
                part.at[turn, pl.ds(0, 1), :], part_in.at[turn, pl.ds(j, 1), :],
                part_send.at[turn, j], part_recv.at[turn, j], peer,
            )
            for j, peer in enumerate(peers)
        ]

    sums = send_part(0, line)
    fold, local = scattered(1)
    local = local + damped
    for copy in sums:
        copy.wait_recv()
    total = total + jnp.sum(part_in[0, : len(line), :], axis=0, keepdims=True)
    part[1, 0:1, :] = total
    sums = send_part(1, plane)
    image = folded(fold, local, 1)
    for copy in sums:
        copy.wait_recv()
    total = total + jnp.sum(part_in[1, : len(plane), :], axis=0, keepdims=True)
    alpha = total[:, 0:1] / total[:, LANES // 2 : LANES // 2 + 1]
    for copy in sent:
        copy.wait_send()
    answer = start + alpha * residual
    left = residual - alpha * image
    for c in range(2):
        for value, target in ((answer, solution_ref), (left, residual_ref)):
            target[10 * c : 10 * c + 10, :] = value[16 * c : 16 * c + 10]


def on_device(sizes, start_params, right_side, prior, matches, pair_first, pair_second, match_counts, send_lists):
    pairs, slots = matches.shape[2], matches.shape[4]
    width = send_lists.shape[3]
    secs, regs, group = sizes
    part_rows = -(-max(group, secs // group * regs) // 8) * 8
    chunks = pairs // LANES
    vmem = pl.BlockSpec(memory_space=pltpu.VMEM)
    hbm = pl.BlockSpec(memory_space=pltpu.HBM)
    field = (FIELD, TILES)
    dma = pltpu.SemaphoreType.DMA
    answer, left = pl.pallas_call(
        functools.partial(kernel, sizes),
        out_shape=(jax.ShapeDtypeStruct((20, TILES), F32),) * 2,
        in_specs=[hbm] * 8,
        out_specs=(vmem, vmem),
        scratch_shapes=[
            pltpu.VMEM((1, pairs), jnp.int32),
            pltpu.VMEM((1, pairs), jnp.int32),
            pltpu.VMEM((chunks, 1, LANES), jnp.int32),
            pltpu.VMEM((2, width), jnp.int32),
            pltpu.VMEM(field, F32),
            pltpu.VMEM(field, F32),
            pltpu.VMEM(field, F32),
            pltpu.VMEM((chunks, LANES, 4, slots), BF16),
            pltpu.VMEM((2, 5, slots, LANES), F32),
            pltpu.VMEM((4 * LANES, 4 * LANES), BF16),
            pltpu.VMEM((chunks, 20, FIELD, LANES), F32),
            pltpu.VMEM((TILES, pairs), BF16),
            pltpu.VMEM((5 * TILES, pairs), BF16),
            pltpu.VMEM((2, FIELD, pairs), F32),
            pltpu.VMEM((2, FIELD, pairs), F32),
            pltpu.VMEM(field, F32),
            pltpu.VMEM((2, 2, width), jnp.int32),
            pltpu.VMEM((2, 4, *field), F32),
            pltpu.VMEM((2, 4, *field), F32),
            pltpu.VMEM((2, 4, *field), F32),
            pltpu.VMEM((2, 8, LANES), F32),
            pltpu.VMEM((2, part_rows, LANES), F32),
            dma((chunks,)),
            dma((4,)),
            dma((6,)),
            dma((2,)),
            dma((2,)),
            dma((2, 4)),
            dma((2, 4)),
            dma((2, 4)),
            dma((2, 4)),
            dma((2, part_rows)),
            dma((2, part_rows)),
        ],
        compiler_params=pltpu.CompilerParams(collective_id=0, has_side_effects=True, vmem_limit_bytes=32 * 2**20),
    )(*[pltpu.with_memory_space_constraint(x, pltpu.HBM) for x in (
        start_params.reshape(20, 1, TILES),
        right_side.reshape(20, 1, TILES),
        prior.reshape(20, 1, TILES),
        matches.reshape(pairs, 4, slots),
        pair_first.reshape(1, pairs),
        pair_second.reshape(1, pairs),
        match_counts.reshape(chunks, 1, LANES),
        send_lists.reshape(2, width),
    )])
    return answer[None, None], left[None, None]


def solution(mesh):
    secs, regs = mesh.shape["sec"], mesh.shape["reg"]
    group = 16 if secs % 16 == 0 else secs
    wide = P("sec", "reg", None, None)
    return jax.shard_map(
        functools.partial(on_device, (secs, regs, group)),
        mesh=mesh,
        in_specs=(
            wide, wide, wide, P("sec", "reg", None, None, None),
            P("sec", "reg", None), P("sec", "reg", None), P("sec", "reg", None), wide,
        ),
        out_specs=(wide, wide),
        check_vma=False,
    )
```

```python
import functools

import jax
import jax.numpy as jnp
from jax import lax
from jax.experimental import pallas as pl
from jax.experimental.pallas import tpu as pltpu
from jax.sharding import PartitionSpec as P

F32, BF16 = jnp.float32, jnp.bfloat16
MESH = pl.DeviceIdType.MESH
EXPONENTS = [(0, 0), (1, 0), (0, 1), (2, 0), (1, 1), (0, 2), (3, 0), (2, 1), (1, 2), (0, 3)]
MOMENTS = [(i, d - i) for d in range(1, 7) for i in range(d, -1, -1)]
TILES = 128
LANES = 128
FIELD = 32
UNROLL = 16
EARLY = 1
FORMED = 3
GROUPS = ((1, 2, 3), (4, 5, 6), (7, 8, 9))


def powers(x, y):
    x2, xy, y2 = x * x, x * y, y * y
    return [None, x, y, x2, xy, y2, x2 * x, x2 * y, y2 * x, y2 * y]


def moments(x, y):
    base = dict(zip(EXPONENTS, powers(x, y)))
    known = dict(base)
    for i, j in MOMENTS:
        if (i, j) not in known:
            a = next(e for e in EXPONENTS[:2:-1] if (i - e[0], j - e[1]) in base)
            known[i, j] = base[a] * base[i - a[0], j - a[1]]
    return [known[e] for e in MOMENTS]


def row_of(n):
    return 16 * (n // 10) + n % 10


def gram_tile(coords, gram, tile, valid, slots):
    zero = jnp.zeros((8, LANES), F32)
    gram[tile, :, 8:16, :] = jnp.zeros((20, 8, LANES), F32)
    gram[tile, :, 24:32, :] = jnp.zeros((20, 8, LANES), F32)

    def sums(terms, which, count):
        def step(i, totals):
            for u in range(UNROLL):
                at = pl.multiple_of((i * UNROLL + u) * 8, 8)
                new = terms(*[coords[c, pl.ds(at, 8), :] for c in which])
                totals = tuple(a + b for a, b in zip(totals, new))
            return totals

        trips = slots // 8 // UNROLL
        totals = step(0, (zero,) * count) if trips == 1 else lax.fori_loop(0, trips, step, (zero,) * count)
        return [jnp.sum(t, axis=0, keepdims=True) for t in totals]

    def put(n, m, row):
        r = row_of(m)
        gram[tile, n, r : r + 1, :] = row

    for side in range(2):
        table = dict(zip(MOMENTS, sums(moments, (2 * side, 2 * side + 1), 27)))
        table[0, 0] = valid
        for n, (i, j) in enumerate(EXPONENTS):
            for m, (k, l) in enumerate(EXPONENTS):
                put(10 * side + n, 10 * side + m, table[i + k, j + l])
        for n, e in enumerate(EXPONENTS):
            if side == 1:
                put(0, 10 + n, table[e])
                put(10 + n, 0, table[e])
            elif n:
                put(10, n, table[e])
                put(n, 10, table[e])
    for some in GROUPS:

        def terms(xa, ya, xb, yb):
            a, b = powers(xa, ya), powers(xb, yb)
            return [a[m] * b[n] for m in some for n in range(1, 10)]

        rows = iter(sums(terms, (0, 1, 2, 3), 9 * len(some)))
        for m in some:
            for n in range(1, 10):
                row = next(rows)
                put(m, 10 + n, row)
                put(10 + n, m, row)


def thirds(x):
    high = x.astype(BF16)
    rest = x - high.astype(F32)
    middle = rest.astype(BF16)
    low = (rest - middle.astype(F32)).astype(BF16)
    return jnp.concatenate([high, middle, low], axis=0)


def joined(x):
    rows = x.shape[0] // 3
    return x[:rows] + x[rows : 2 * rows] + x[2 * rows :]


def matmul(a, b):
    return lax.dot_general(a, b, (((1,), (0,)), ((), ())), preferred_element_type=F32)


def matmul_t(a, b):
    return lax.dot_general(a, b, (((1,), (1,)), ((), ())), preferred_element_type=F32)


def kernel(
    sizes, params_hbm, side_hbm, prior_hbm, matches_hbm, first_hbm, second_hbm, count_hbm, lists_hbm,
    solution_ref, residual_ref,
    first_ref, second_ref, count_ref, lists_ref, params, side, prior, points, coords, sort_ref, gram, own_hot, other_hot, z_ref,
    y_ref, direction, lists_in, halo_in, fold_out, fold_in, part, part_in,
    load_sem, small_sem, field_sem, list_send, list_recv, halo_send, halo_recv, fold_send, fold_recv, part_send, part_recv,
):
    secs, regs, group = sizes
    sec, reg = lax.axis_index("sec"), lax.axis_index("reg")
    pairs = first_hbm.shape[1]
    slots = matches_hbm.shape[2]
    chunks = pairs // LANES
    rows = secs // group

    def device(by_sec, by_reg):
        return (lax.rem(sec + by_sec + secs, secs), lax.rem(reg + by_reg + regs, regs))

    borrowers = [device(1, 0), device(2, 0), device(0, 1), device(0, -1)]
    owners = [device(-1, 0), device(-2, 0), device(0, -1), device(0, 1)]
    base, place = group * (sec // group), lax.rem(sec, group)
    line = [(base + lax.rem(place + j, group), reg) for j in sorted(range(1, group), key=lambda j: abs(2 * j - group))]
    hops = [(min(a, rows - a) + min(b, regs - b), a, b) for a in range(rows) for b in range(regs) if a or b]
    plane = [
        (lax.rem(sec // group + a, rows) * group + place, lax.rem(reg + b, regs)) for _, a, b in sorted(hops, reverse=True)
    ]

    loads = []
    for i in range(chunks):
        loads.append(pltpu.make_async_copy(matches_hbm.at[pl.ds(i * LANES, LANES)], points.at[i], load_sem.at[i]))
    fields = [
        pltpu.make_async_copy(source.at[:, :, 0, :], target.at[:, pl.ds(0, 10), :], field_sem.at[i])
        for i, (source, target) in enumerate(((params_hbm, params), (side_hbm, side), (prior_hbm, prior)))
    ]
    for target in (params, side, prior):
        target[:, 10:16, :] = jnp.zeros((2, 6, TILES), F32)
    small = [
        pltpu.make_async_copy(source, target, small_sem.at[i])
        for i, (source, target) in enumerate(
            ((lists_hbm, lists_ref), (count_hbm, count_ref), (first_hbm, first_ref), (second_hbm, second_ref))
        )
    ]
    for copy in loads[:1] + small[:1] + fields[:1] + small[1:2] + loads[1:] + small[2:] + fields[1:]:
        copy.start()

    halo_in[...] = jnp.zeros_like(halo_in)
    fold_in[...] = jnp.zeros_like(fold_in)
    lists_in[...] = jnp.zeros_like(lists_in)
    barrier = pltpu.get_barrier_semaphore()
    for peer in borrowers + owners[:2] + line + plane:
        pl.semaphore_signal(barrier, inc=1, device_id=peer, device_id_type=MESH)

    above = [sec < secs - 1, sec < secs - 2, reg < regs - 1, reg > 0]
    below = [sec > 0, sec > 1, reg > 0, reg < regs - 1]
    sent = []

    def send(source, target, send_sem, recv_sem, peer, sends=None, receives=None):
        copy = pltpu.make_async_remote_copy(
            src_ref=source, dst_ref=target, send_sem=send_sem, recv_sem=recv_sem, device_id=peer, device_id_type=MESH
        )
        if sends is None:
            copy.start()
            sent.append(copy.wait_send)
            return copy.wait_recv
        pl.when(sends)(copy.start)
        sent.append(lambda: pl.when(sends)(copy.wait_send))
        return lambda: pl.when(receives)(copy.wait_recv)

    def send_halo(source, turn):
        return [
            send(
                source.at[:, pl.ds(0, 10), :], halo_in.at[turn, i, :, pl.ds(0, 10), :], halo_send.at[turn, i], halo_recv.at[turn, i], borrowers[i], above[i], below[i]
            )
            for i in range(4)
        ]

    def send_fold(turn):
        return [
            send(
                fold_out.at[turn, i, :, pl.ds(0, 10), :], fold_in.at[turn, i, :, pl.ds(0, 10), :], fold_send.at[turn, i], fold_recv.at[turn, i], owners[i],
                below[i], above[i],
            )
            for i in range(4)
        ]

    r = lax.broadcasted_iota(jnp.int32, (4 * LANES, 4 * LANES), 0)
    s = lax.broadcasted_iota(jnp.int32, (4 * LANES, 4 * LANES), 1)
    sort_ref[...] = jnp.where(r == 4 * lax.rem(s, LANES) + s // LANES, 1.0, 0.0).astype(BF16)
    slot = lax.broadcasted_iota(jnp.int32, (slots, LANES), 0)

    def turn(tile, to):
        turned = lax.dot_general(
            points[tile].reshape(4 * LANES, slots), sort_ref[...], (((0,), (0,)), ((), ())), preferred_element_type=F32
        )
        live = slot < count_ref[tile]
        for c in range(4):
            coords[to, c] = jnp.where(live, turned[:, c * LANES : (c + 1) * LANES], 0.0)
        coords[to, 4] = jnp.where(live, 1.0, 0.0)

    def gram_of(tile, at):
        gram_tile(coords.at[at], gram, tile, count_ref[tile].astype(F32), slots)

    def form(tile):
        at = lax.rem(tile, 2)
        turn(tile, at)
        gram_of(tile, at)

    for copy in small[1:] + fields[1:] + loads:
        copy.wait()
    pl.loop(0, EARLY)(form)
    for copy in fields[:1] + small[:1]:
        copy.wait()
    pl.semaphore_wait(barrier, 6 + len(line) + len(plane))
    halo = send_halo(params, 0)
    borders = [
        send(lists_ref, lists_in.at[0], list_send.at[0], list_recv.at[0], borrowers[2], above[2], below[2]),
        send(lists_ref, lists_in.at[1], list_send.at[1], list_recv.at[1], borrowers[3], above[3], below[3]),
    ]


    pl.loop(EARLY, FORMED)(form)
    for tile in range(FORMED, chunks):
        turn(tile, tile % 2)

    for arrived in borders:
        arrived()
    second = second_ref[...]
    width = lists_ref.shape[1]
    index = jnp.where(second < 3 * TILES, second, -1).astype(F32)
    for i in range(2):
        start = 3 * TILES + i * width
        spot = lax.broadcasted_iota(jnp.int32, (width, pairs), 0) + start
        named = jnp.where(spot == second, 1.0, 0.0).astype(BF16)
        tile_at = matmul((lists_in[i] + 1).astype(F32).astype(BF16), named)[1 - i : 2 - i]
        index = jnp.where(tile_at > 0, tile_at + float((3 + i) * TILES - 1), index)
    index = index.astype(jnp.int32)
    column = lax.broadcasted_iota(jnp.int32, (TILES, pairs), 0)
    own_hot[...] = jnp.where(column == first_ref[...], 1.0, 0.0).astype(BF16)
    for i in range(5):
        other_hot[i * TILES : (i + 1) * TILES, :] = jnp.where(column + i * TILES == index, -1.0, 0.0).astype(BF16)

    def gathered(field, turn, halo):
        mine = thirds(field)
        own = joined(matmul(mine, own_hot[...]))
        other = matmul(mine, other_hot[:TILES, :])
        for arrived in halo:
            arrived()
        others = jnp.concatenate([thirds(halo_in[turn, i].reshape(FIELD, TILES)) for i in range(4)], axis=1)
        other = joined(other + matmul(others, other_hot[TILES:, :]))
        z_ref[0] = own
        z_ref[1] = other

    scale = 2.0 / slots

    def products(tiles):
        for tile in range(tiles):
            at = slice(tile * LANES, (tile + 1) * LANES)
            totals = [None, None]
            for n in range(20):
                block = gram[tile, n]
                for c in range(2):
                    row = 16 * c + n % 10
                    term = block * z_ref[n // 10, row : row + 1, at]
                    totals[c] = term if totals[c] is None else totals[c] + term
            for c in range(2):
                for half in range(2):
                    y_ref[half, 16 * c : 16 * c + 16, at] = totals[c][16 * half : 16 * half + 16]

    def direct(tile):
        at = slice(tile * LANES, (tile + 1) * LANES)
        points_of = coords.at[tile % 2]
        for c in range(2):
            z = [[z_ref[half, 16 * c + m : 16 * c + m + 1, at] for m in range(10)] for half in range(2)]
            constant = z[0][0] + z[1][0]

            def step(i, totals):
                for u in range(UNROLL):
                    here = pl.multiple_of((i * UNROLL + u) * 8, 8)
                    xa, ya, xb, yb, live = [points_of[d, pl.ds(here, 8), :] for d in range(5)]
                    basis = powers(xa, ya)[1:] + powers(xb, yb)[1:]
                    first_half, second_half = constant + z[0][1] * xa, z[1][1] * xb
                    for m in range(1, 9):
                        first_half = first_half + z[0][m + 1] * basis[m]
                        second_half = second_half + z[1][m + 1] * basis[9 + m]
                    mismatch = (first_half + second_half) * live
                    totals = (totals[0] + mismatch,) + tuple(t + b * mismatch for t, b in zip(totals[1:], basis))
                return totals

            totals = lax.fori_loop(0, slots // 8 // UNROLL, step, (jnp.zeros((8, LANES), F32),) * 19)
            totals = [jnp.sum(t, axis=0, keepdims=True) for t in totals]
            for half in range(2):
                y_ref[half, 16 * c : 16 * c + 1, at] = totals[0]
                for m in range(1, 10):
                    y_ref[half, 16 * c + m : 16 * c + m + 1, at] = totals[9 * half + m]

    def scattered(turn):
        own, other = y_ref[0] * scale, y_ref[1] * scale
        others = thirds(other)
        lent = joined(matmul_t(others, other_hot[TILES:, :]))
        for i in range(4):
            fold_out[turn, i] = lent[:, i * TILES : (i + 1) * TILES].reshape(2, FIELD // 2, TILES)
        fold = send_fold(turn)
        local = joined(matmul_t(thirds(own), own_hot[...]) + matmul_t(others, other_hot[:TILES, :]))
        return fold, local

    def folded(fold, local, turn):
        for arrived in fold:
            arrived()
        return local + jnp.sum(fold_in[turn], axis=0).reshape(FIELD, TILES)

    start = params[...].reshape(FIELD, TILES)
    gathered(start, 0, halo)
    for c in range(2):
        for half in range(2):
            y_ref[half, 16 * c + 10 : 16 * c + 16, :] = jnp.zeros((6, pairs), F32)
    for tile in range(FORMED, chunks):
        direct(tile)
    products(FORMED)
    fold, local = scattered(0)
    for tile in range(FORMED, chunks - 1):
        gram_of(tile, tile % 2)
    local = local + prior[...].reshape(FIELD, TILES) * start
    residual = side[...].reshape(FIELD, TILES) - folded(fold, local, 0)

    direction[...] = residual.reshape(2, FIELD // 2, TILES)
    halo = send_halo(direction, 1)
    gram_of(chunks - 1, (chunks - 1) % 2)
    squares = jnp.sum(residual * residual, keepdims=True)
    damped = prior[...].reshape(FIELD, TILES) * residual
    gathered(residual, 1, halo)
    products(chunks)
    energy = scale * jnp.sum(y_ref[0] * z_ref[0] + y_ref[1] * z_ref[1], keepdims=True) + jnp.sum(damped * residual, keepdims=True)
    lane = lax.broadcasted_iota(jnp.int32, (1, LANES), 1)
    total = jnp.where(lane < LANES // 2, squares, energy)
    part[0, 0:1, :] = total

    def send_part(turn, peers):
        return [
            send(
                part.at[turn, pl.ds(0, 1), :], part_in.at[turn, pl.ds(j, 1), :],
                part_send.at[turn, j], part_recv.at[turn, j], peer,
            )
            for j, peer in enumerate(peers)
        ]

    sums = send_part(0, line)
    fold, local = scattered(1)
    local = local + damped
    for arrived in sums:
        arrived()
    total = total + jnp.sum(part_in[0, : len(line), :], axis=0, keepdims=True)
    part[1, 0:1, :] = total
    sums = send_part(1, plane)
    image = folded(fold, local, 1)
    for arrived in sums:
        arrived()
    total = total + jnp.sum(part_in[1, : len(plane), :], axis=0, keepdims=True)
    alpha = total[:, 0:1] / total[:, LANES // 2 : LANES // 2 + 1]
    for left_here in sent:
        left_here()
    answer = start + alpha * residual
    left = residual - alpha * image
    for c in range(2):
        for value, target in ((answer, solution_ref), (left, residual_ref)):
            target[10 * c : 10 * c + 10, :] = value[16 * c : 16 * c + 10]


def on_device(sizes, start_params, right_side, prior, matches, pair_first, pair_second, match_counts, send_lists):
    pairs, slots = matches.shape[2], matches.shape[4]
    width = send_lists.shape[3]
    secs, regs, group = sizes
    part_rows = -(-max(group, secs // group * regs) // 8) * 8
    chunks = pairs // LANES
    vmem = pl.BlockSpec(memory_space=pltpu.VMEM)
    hbm = pl.BlockSpec(memory_space=pltpu.HBM)
    field, split = (FIELD, TILES), (2, FIELD // 2, TILES)
    dma = pltpu.SemaphoreType.DMA
    answer, left = pl.pallas_call(
        functools.partial(kernel, sizes),
        out_shape=(jax.ShapeDtypeStruct((20, TILES), F32),) * 2,
        in_specs=[hbm] * 8,
        out_specs=(vmem, vmem),
        scratch_shapes=[
            pltpu.VMEM((1, pairs), jnp.int32),
            pltpu.VMEM((1, pairs), jnp.int32),
            pltpu.VMEM((chunks, 1, LANES), jnp.int32),
            pltpu.VMEM((2, width), jnp.int32),
            pltpu.VMEM(split, F32),
            pltpu.VMEM(split, F32),
            pltpu.VMEM(split, F32),
            pltpu.VMEM((chunks, LANES, 4, slots), BF16),
            pltpu.VMEM((2, 5, slots, LANES), F32),
            pltpu.VMEM((4 * LANES, 4 * LANES), BF16),
            pltpu.VMEM((chunks, 20, FIELD, LANES), F32),
            pltpu.VMEM((TILES, pairs), BF16),
            pltpu.VMEM((5 * TILES, pairs), BF16),
            pltpu.VMEM((2, FIELD, pairs), F32),
            pltpu.VMEM((2, FIELD, pairs), F32),
            pltpu.VMEM(split, F32),
            pltpu.VMEM((2, 2, width), jnp.int32),
            pltpu.VMEM((2, 4, *split), F32),
            pltpu.VMEM((2, 4, *split), F32),
            pltpu.VMEM((2, 4, *split), F32),
            pltpu.VMEM((2, 8, LANES), F32),
            pltpu.VMEM((2, part_rows, LANES), F32),
            dma((chunks,)),
            dma((4,)),
            dma((3,)),
            dma((2,)),
            dma((2,)),
            dma((2, 4)),
            dma((2, 4)),
            dma((2, 4)),
            dma((2, 4)),
            dma((2, part_rows)),
            dma((2, part_rows)),
        ],
        compiler_params=pltpu.CompilerParams(collective_id=0, has_side_effects=True, vmem_limit_bytes=32 * 2**20),
    )(*[pltpu.with_memory_space_constraint(x, pltpu.HBM) for x in (
        start_params.reshape(2, 10, 1, TILES),
        right_side.reshape(2, 10, 1, TILES),
        prior.reshape(2, 10, 1, TILES),
        matches.reshape(pairs, 4, slots),
        pair_first.reshape(1, pairs),
        pair_second.reshape(1, pairs),
        match_counts.reshape(chunks, 1, LANES),
        send_lists.reshape(2, width),
    )])
    return answer[None, None], left[None, None]


def solution(mesh):
    secs, regs = mesh.shape["sec"], mesh.shape["reg"]
    group = 16 if secs % 16 == 0 else secs
    wide = P("sec", "reg", None, None)
    return jax.shard_map(
        functools.partial(on_device, (secs, regs, group)),
        mesh=mesh,
        in_specs=(
            wide, wide, wide, P("sec", "reg", None, None, None),
            P("sec", "reg", None), P("sec", "reg", None), P("sec", "reg", None), wide,
        ),
        out_specs=(wide, wide),
        check_vma=False,
    )
```

```python
import functools

import jax
import jax.numpy as jnp
from jax import lax
from jax.experimental import pallas as pl
from jax.experimental.pallas import tpu as pltpu
from jax.sharding import PartitionSpec as P

F32, BF16 = jnp.float32, jnp.bfloat16
MESH = pl.DeviceIdType.MESH
EXPONENTS = [(0, 0), (1, 0), (0, 1), (2, 0), (1, 1), (0, 2), (3, 0), (2, 1), (1, 2), (0, 3)]
MOMENTS = [(i, d - i) for d in range(1, 7) for i in range(d, -1, -1)]
TILES = 128
LANES = 128
FIELD = 32
UNROLL = 16
EARLY = 1
FORMED = 3
GROUPS = ((1, 2, 3), (4, 5, 6), (7, 8, 9))


def powers(x, y):
    x2, xy, y2 = x * x, x * y, y * y
    return [None, x, y, x2, xy, y2, x2 * x, x2 * y, y2 * x, y2 * y]


def moments(x, y):
    base = dict(zip(EXPONENTS, powers(x, y)))
    known = dict(base)
    for i, j in MOMENTS:
        if (i, j) not in known:
            a = next(e for e in EXPONENTS[:2:-1] if (i - e[0], j - e[1]) in base)
            known[i, j] = base[a] * base[i - a[0], j - a[1]]
    return [known[e] for e in MOMENTS]


def row_of(n):
    return 16 * (n // 10) + n % 10


def gram_tile(coords, gram, tile, valid, slots):
    zero = jnp.zeros((8, LANES), F32)
    gram[tile, :, 8:16, :] = jnp.zeros((20, 8, LANES), F32)
    gram[tile, :, 24:32, :] = jnp.zeros((20, 8, LANES), F32)

    def sums(terms, which, count):
        def step(i, totals):
            for u in range(UNROLL):
                at = pl.multiple_of((i * UNROLL + u) * 8, 8)
                new = terms(*[coords[c, pl.ds(at, 8), :] for c in which])
                totals = tuple(a + b for a, b in zip(totals, new))
            return totals

        trips = slots // 8 // UNROLL
        totals = step(0, (zero,) * count) if trips == 1 else lax.fori_loop(0, trips, step, (zero,) * count)
        return [jnp.sum(t, axis=0, keepdims=True) for t in totals]

    def put(n, m, row):
        r = row_of(m)
        gram[tile, n, r : r + 1, :] = row

    for side in range(2):
        table = dict(zip(MOMENTS, sums(moments, (2 * side, 2 * side + 1), 27)))
        table[0, 0] = valid
        for n, (i, j) in enumerate(EXPONENTS):
            for m, (k, l) in enumerate(EXPONENTS):
                put(10 * side + n, 10 * side + m, table[i + k, j + l])
        for n, e in enumerate(EXPONENTS):
            if side == 1:
                put(0, 10 + n, table[e])
                put(10 + n, 0, table[e])
            elif n:
                put(10, n, table[e])
                put(n, 10, table[e])
    for some in GROUPS:

        def terms(xa, ya, xb, yb):
            a, b = powers(xa, ya), powers(xb, yb)
            return [a[m] * b[n] for m in some for n in range(1, 10)]

        rows = iter(sums(terms, (0, 1, 2, 3), 9 * len(some)))
        for m in some:
            for n in range(1, 10):
                row = next(rows)
                put(m, 10 + n, row)
                put(10 + n, m, row)


def thirds(x):
    high = x.astype(BF16)
    rest = x - high.astype(F32)
    middle = rest.astype(BF16)
    low = (rest - middle.astype(F32)).astype(BF16)
    return jnp.concatenate([high, middle, low], axis=0)


def joined(x):
    rows = x.shape[0] // 3
    return x[:rows] + x[rows : 2 * rows] + x[2 * rows :]


def matmul(a, b):
    return lax.dot_general(a, b, (((1,), (0,)), ((), ())), preferred_element_type=F32)


def matmul_t(a, b):
    return lax.dot_general(a, b, (((1,), (1,)), ((), ())), preferred_element_type=F32)


def kernel(
    sizes, params_hbm, side_hbm, prior_hbm, matches_hbm, first_hbm, second_hbm, count_hbm, lists_hbm,
    solution_ref, residual_ref,
    first_ref, second_ref, count_ref, lists_ref, params, side, prior, points, coords, sort_ref, gram, own_hot, other_hot, z_ref,
    y_ref, direction, lists_in, halo_in, fold_out, fold_in, part, part_in,
    load_sem, small_sem, field_sem, list_send, list_recv, halo_send, halo_recv, fold_send, fold_recv, part_send, part_recv,
):
    secs, regs, group = sizes
    sec, reg = lax.axis_index("sec"), lax.axis_index("reg")
    pairs = first_hbm.shape[1]
    slots = matches_hbm.shape[2]
    chunks = pairs // LANES
    rows = secs // group

    loads = []
    for i in range(chunks):
        loads.append(pltpu.make_async_copy(matches_hbm.at[pl.ds(i * LANES, LANES)], points.at[i], load_sem.at[i]))
    fields = [
        pltpu.make_async_copy(source.at[:, :, 0, :], target.at[:, pl.ds(0, 10), :], field_sem.at[i])
        for i, (source, target) in enumerate(((params_hbm, params), (side_hbm, side), (prior_hbm, prior)))
    ]
    for target in (params, side, prior):
        target[:, 10:16, :] = jnp.zeros((2, 6, TILES), F32)
    small = [
        pltpu.make_async_copy(source, target, small_sem.at[i])
        for i, (source, target) in enumerate(
            ((lists_hbm, lists_ref), (count_hbm, count_ref), (first_hbm, first_ref), (second_hbm, second_ref))
        )
    ]
    for copy in loads[:1] + small[:1] + fields[:1] + small[1:2] + loads[1:] + small[2:] + fields[1:]:
        copy.start()

    def device(by_sec, by_reg):
        return (lax.rem(sec + by_sec + secs, secs), lax.rem(reg + by_reg + regs, regs))

    borrowers = [device(1, 0), device(2, 0), device(0, 1), device(0, -1)]
    owners = [device(-1, 0), device(-2, 0), device(0, -1), device(0, 1)]
    base, place = group * (sec // group), lax.rem(sec, group)
    line = [(base + lax.rem(place + j, group), reg) for j in sorted(range(1, group), key=lambda j: abs(2 * j - group))]
    hops = [(min(a, rows - a) + min(b, regs - b), a, b) for a in range(rows) for b in range(regs) if a or b]
    plane = [
        (lax.rem(sec // group + a, rows) * group + place, lax.rem(reg + b, regs)) for _, a, b in sorted(hops, reverse=True)
    ]

    halo_in[...] = jnp.zeros_like(halo_in)
    fold_in[...] = jnp.zeros_like(fold_in)
    lists_in[...] = jnp.zeros_like(lists_in)
    barrier = pltpu.get_barrier_semaphore()
    for peer in borrowers + owners[:2] + line + plane:
        pl.semaphore_signal(barrier, inc=1, device_id=peer, device_id_type=MESH)

    above = [sec < secs - 1, sec < secs - 2, reg < regs - 1, reg > 0]
    below = [sec > 0, sec > 1, reg > 0, reg < regs - 1]
    sent = []

    def send(source, target, send_sem, recv_sem, peer, sends=None, receives=None):
        copy = pltpu.make_async_remote_copy(
            src_ref=source, dst_ref=target, send_sem=send_sem, recv_sem=recv_sem, device_id=peer, device_id_type=MESH
        )
        if sends is None:
            copy.start()
            sent.append(copy.wait_send)
            return copy.wait_recv
        pl.when(sends)(copy.start)
        sent.append(lambda: pl.when(sends)(copy.wait_send))
        return lambda: pl.when(receives)(copy.wait_recv)

    def send_halo(source, turn):
        return [
            send(
                source.at[:, pl.ds(0, 10), :], halo_in.at[turn, i, :, pl.ds(0, 10), :], halo_send.at[turn, i], halo_recv.at[turn, i], borrowers[i], above[i], below[i]
            )
            for i in range(4)
        ]

    def send_fold(turn):
        return [
            send(
                fold_out.at[turn, i, :, pl.ds(0, 10), :], fold_in.at[turn, i, :, pl.ds(0, 10), :], fold_send.at[turn, i], fold_recv.at[turn, i], owners[i],
                below[i], above[i],
            )
            for i in range(4)
        ]

    r = lax.broadcasted_iota(jnp.int32, (4 * LANES, 4 * LANES), 0)
    s = lax.broadcasted_iota(jnp.int32, (4 * LANES, 4 * LANES), 1)
    sort_ref[...] = jnp.where(r == 4 * lax.rem(s, LANES) + s // LANES, 1.0, 0.0).astype(BF16)
    slot = lax.broadcasted_iota(jnp.int32, (slots, LANES), 0)

    def turn(tile, to):
        turned = lax.dot_general(
            points[tile].reshape(4 * LANES, slots), sort_ref[...], (((0,), (0,)), ((), ())), preferred_element_type=F32
        )
        live = slot < count_ref[tile]
        for c in range(4):
            coords[to, c] = jnp.where(live, turned[:, c * LANES : (c + 1) * LANES], 0.0)
        coords[to, 4] = jnp.where(live, 1.0, 0.0)

    def gram_of(tile, at):
        gram_tile(coords.at[at], gram, tile, count_ref[tile].astype(F32), slots)

    def form(tile):
        at = lax.rem(tile, 2)
        turn(tile, at)
        gram_of(tile, at)

    for copy in small[1:2] + loads[:1]:
        copy.wait()
    pl.loop(0, EARLY)(form)
    for copy in loads[1:] + small[2:] + fields[1:]:
        copy.wait()
    for copy in fields[:1] + small[:1]:
        copy.wait()
    pl.semaphore_wait(barrier, 6 + len(line) + len(plane))
    halo = send_halo(params, 0)
    borders = [
        send(lists_ref, lists_in.at[0], list_send.at[0], list_recv.at[0], borrowers[2], above[2], below[2]),
        send(lists_ref, lists_in.at[1], list_send.at[1], list_recv.at[1], borrowers[3], above[3], below[3]),
    ]


    pl.loop(EARLY, FORMED)(form)
    for tile in range(FORMED, chunks):
        turn(tile, tile % 2)

    for arrived in borders:
        arrived()
    second = second_ref[...]
    width = lists_ref.shape[1]
    index = jnp.where(second < 3 * TILES, second, -1).astype(F32)
    for i in range(2):
        start = 3 * TILES + i * width
        spot = lax.broadcasted_iota(jnp.int32, (width, pairs), 0) + start
        named = jnp.where(spot == second, 1.0, 0.0).astype(BF16)
        tile_at = matmul((lists_in[i] + 1).astype(F32).astype(BF16), named)[1 - i : 2 - i]
        index = jnp.where(tile_at > 0, tile_at + float((3 + i) * TILES - 1), index)
    index = index.astype(jnp.int32)
    column = lax.broadcasted_iota(jnp.int32, (TILES, pairs), 0)
    own_hot[...] = jnp.where(column == first_ref[...], 1.0, 0.0).astype(BF16)
    for i in range(5):
        other_hot[i * TILES : (i + 1) * TILES, :] = jnp.where(column == index - i * TILES, -1.0, 0.0).astype(BF16)

    def gathered(field, turn, halo):
        mine = thirds(field)
        own = joined(matmul(mine, own_hot[...]))
        other = matmul(mine, other_hot[:TILES, :])
        for arrived in halo:
            arrived()
        others = jnp.concatenate([thirds(halo_in[turn, i].reshape(FIELD, TILES)) for i in range(4)], axis=1)
        other = joined(other + matmul(others, other_hot[TILES:, :]))
        z_ref[0] = own
        z_ref[1] = other

    scale = 2.0 / slots

    def products(tiles):
        for tile in range(tiles):
            at = slice(tile * LANES, (tile + 1) * LANES)
            totals = [None, None]
            for n in range(20):
                block = gram[tile, n]
                for c in range(2):
                    row = 16 * c + n % 10
                    term = block * z_ref[n // 10, row : row + 1, at]
                    totals[c] = term if totals[c] is None else totals[c] + term
            for c in range(2):
                for half in range(2):
                    y_ref[half, 16 * c : 16 * c + 16, at] = totals[c][16 * half : 16 * half + 16]

    def direct(tile):
        at = slice(tile * LANES, (tile + 1) * LANES)
        points_of = coords.at[tile % 2]
        for c in range(2):
            z = [[z_ref[half, 16 * c + m : 16 * c + m + 1, at] for m in range(10)] for half in range(2)]
            constant = z[0][0] + z[1][0]

            def step(i, totals):
                for u in range(UNROLL):
                    here = pl.multiple_of((i * UNROLL + u) * 8, 8)
                    xa, ya, xb, yb, live = [points_of[d, pl.ds(here, 8), :] for d in range(5)]
                    basis = powers(xa, ya)[1:] + powers(xb, yb)[1:]
                    first_half, second_half = constant + z[0][1] * xa, z[1][1] * xb
                    for m in range(1, 9):
                        first_half = first_half + z[0][m + 1] * basis[m]
                        second_half = second_half + z[1][m + 1] * basis[9 + m]
                    mismatch = (first_half + second_half) * live
                    totals = (totals[0] + mismatch,) + tuple(t + b * mismatch for t, b in zip(totals[1:], basis))
                return totals

            totals = lax.fori_loop(0, slots // 8 // UNROLL, step, (jnp.zeros((8, LANES), F32),) * 19)
            totals = [jnp.sum(t, axis=0, keepdims=True) for t in totals]
            for half in range(2):
                y_ref[half, 16 * c : 16 * c + 1, at] = totals[0]
                for m in range(1, 10):
                    y_ref[half, 16 * c + m : 16 * c + m + 1, at] = totals[9 * half + m]

    def scattered(turn):
        own, other = y_ref[0] * scale, y_ref[1] * scale
        others = thirds(other)
        lent = joined(matmul_t(others, other_hot[TILES:, :]))
        for i in range(4):
            fold_out[turn, i] = lent[:, i * TILES : (i + 1) * TILES].reshape(2, FIELD // 2, TILES)
        fold = send_fold(turn)
        local = joined(matmul_t(thirds(own), own_hot[...]) + matmul_t(others, other_hot[:TILES, :]))
        return fold, local

    def folded(fold, local, turn):
        for arrived in fold:
            arrived()
        return local + jnp.sum(fold_in[turn], axis=0).reshape(FIELD, TILES)

    start = params[...].reshape(FIELD, TILES)
    gathered(start, 0, halo)
    for c in range(2):
        for half in range(2):
            y_ref[half, 16 * c + 10 : 16 * c + 16, :] = jnp.zeros((6, pairs), F32)
    for tile in range(FORMED, chunks):
        direct(tile)
    products(FORMED)
    fold, local = scattered(0)
    for tile in range(FORMED, chunks - 1):
        gram_of(tile, tile % 2)
    local = local + prior[...].reshape(FIELD, TILES) * start
    residual = side[...].reshape(FIELD, TILES) - folded(fold, local, 0)

    direction[...] = residual.reshape(2, FIELD // 2, TILES)
    halo = send_halo(direction, 1)
    gram_of(chunks - 1, (chunks - 1) % 2)
    squares = jnp.sum(residual * residual, keepdims=True)
    damped = prior[...].reshape(FIELD, TILES) * residual
    gathered(residual, 1, halo)
    products(chunks)
    energy = scale * jnp.sum(y_ref[0] * z_ref[0] + y_ref[1] * z_ref[1], keepdims=True) + jnp.sum(damped * residual, keepdims=True)
    lane = lax.broadcasted_iota(jnp.int32, (1, LANES), 1)
    total = jnp.where(lane < LANES // 2, squares, energy)
    part[0, 0:1, :] = total

    def send_part(turn, peers):
        return [
            send(
                part.at[turn, pl.ds(0, 1), :], part_in.at[turn, pl.ds(j, 1), :],
                part_send.at[turn, j], part_recv.at[turn, j], peer,
            )
            for j, peer in enumerate(peers)
        ]

    sums = send_part(0, line)
    fold, local = scattered(1)
    local = local + damped
    for arrived in sums:
        arrived()
    total = total + jnp.sum(part_in[0, : len(line), :], axis=0, keepdims=True)
    part[1, 0:1, :] = total
    sums = send_part(1, plane)
    image = folded(fold, local, 1)
    for left_here in sent:
        left_here()
    for arrived in sums:
        arrived()
    total = total + jnp.sum(part_in[1, : len(plane), :], axis=0, keepdims=True)
    alpha = total[:, 0:1] / total[:, LANES // 2 : LANES // 2 + 1]
    answer = start + alpha * residual
    left = residual - alpha * image
    for c in range(2):
        for value, target in ((answer, solution_ref), (left, residual_ref)):
            target[10 * c : 10 * c + 10, :] = value[16 * c : 16 * c + 10]


def on_device(sizes, start_params, right_side, prior, matches, pair_first, pair_second, match_counts, send_lists):
    pairs, slots = matches.shape[2], matches.shape[4]
    width = send_lists.shape[3]
    secs, regs, group = sizes
    part_rows = -(-max(group, secs // group * regs) // 8) * 8
    chunks = pairs // LANES
    vmem = pl.BlockSpec(memory_space=pltpu.VMEM)
    hbm = pl.BlockSpec(memory_space=pltpu.HBM)
    field, split = (FIELD, TILES), (2, FIELD // 2, TILES)
    dma = pltpu.SemaphoreType.DMA
    answer, left = pl.pallas_call(
        functools.partial(kernel, sizes),
        out_shape=(jax.ShapeDtypeStruct((20, TILES), F32),) * 2,
        in_specs=[hbm] * 8,
        out_specs=(vmem, vmem),
        scratch_shapes=[
            pltpu.VMEM((1, pairs), jnp.int32),
            pltpu.VMEM((1, pairs), jnp.int32),
            pltpu.VMEM((chunks, 1, LANES), jnp.int32),
            pltpu.VMEM((2, width), jnp.int32),
            pltpu.VMEM(split, F32),
            pltpu.VMEM(split, F32),
            pltpu.VMEM(split, F32),
            pltpu.VMEM((chunks, LANES, 4, slots), BF16),
            pltpu.VMEM((2, 5, slots, LANES), F32),
            pltpu.VMEM((4 * LANES, 4 * LANES), BF16),
            pltpu.VMEM((chunks, 20, FIELD, LANES), F32),
            pltpu.VMEM((TILES, pairs), BF16),
            pltpu.VMEM((5 * TILES, pairs), BF16),
            pltpu.VMEM((2, FIELD, pairs), F32),
            pltpu.VMEM((2, FIELD, pairs), F32),
            pltpu.VMEM(split, F32),
            pltpu.VMEM((2, 2, width), jnp.int32),
            pltpu.VMEM((2, 4, *split), F32),
            pltpu.VMEM((2, 4, *split), F32),
            pltpu.VMEM((2, 4, *split), F32),
            pltpu.VMEM((2, 8, LANES), F32),
            pltpu.VMEM((2, part_rows, LANES), F32),
            dma((chunks,)),
            dma((4,)),
            dma((3,)),
            dma((2,)),
            dma((2,)),
            dma((2, 4)),
            dma((2, 4)),
            dma((2, 4)),
            dma((2, 4)),
            dma((2, part_rows)),
            dma((2, part_rows)),
        ],
        compiler_params=pltpu.CompilerParams(collective_id=0, has_side_effects=True, vmem_limit_bytes=32 * 2**20),
    )(*[pltpu.with_memory_space_constraint(x, pltpu.HBM) for x in (
        start_params.reshape(2, 10, 1, TILES),
        right_side.reshape(2, 10, 1, TILES),
        prior.reshape(2, 10, 1, TILES),
        matches.reshape(pairs, 4, slots),
        pair_first.reshape(1, pairs),
        pair_second.reshape(1, pairs),
        match_counts.reshape(chunks, 1, LANES),
        send_lists.reshape(2, width),
    )])
    return answer[None, None], left[None, None]


def solution(mesh):
    secs, regs = mesh.shape["sec"], mesh.shape["reg"]
    group = 16 if secs % 16 == 0 else secs
    wide = P("sec", "reg", None, None)
    return jax.shard_map(
        functools.partial(on_device, (secs, regs, group)),
        mesh=mesh,
        in_specs=(
            wide, wide, wide, P("sec", "reg", None, None, None),
            P("sec", "reg", None), P("sec", "reg", None), P("sec", "reg", None), wide,
        ),
        out_specs=(wide, wide),
        check_vma=False,
    )
```

```python
import functools

import jax
import jax.numpy as jnp
from jax import lax
from jax.experimental import pallas as pl
from jax.experimental.pallas import tpu as pltpu
from jax.sharding import PartitionSpec as P

F32, BF16 = jnp.float32, jnp.bfloat16
MESH = pl.DeviceIdType.MESH
EXPONENTS = [(0, 0), (1, 0), (0, 1), (2, 0), (1, 1), (0, 2), (3, 0), (2, 1), (1, 2), (0, 3)]
MOMENTS = [(i, d - i) for d in range(1, 7) for i in range(d, -1, -1)]
TILES = 128
LANES = 128
FIELD = 32
UNROLL = 16
EARLY = 1
FORMED = 2
GROUPS = ((1, 2, 3), (4, 5, 6), (7, 8, 9))


def powers(x, y):
    x2, xy, y2 = x * x, x * y, y * y
    return [None, x, y, x2, xy, y2, x2 * x, x2 * y, y2 * x, y2 * y]


def moments(x, y):
    base = dict(zip(EXPONENTS, powers(x, y)))
    known = dict(base)
    for i, j in MOMENTS:
        if (i, j) not in known:
            a = next(e for e in EXPONENTS[:2:-1] if (i - e[0], j - e[1]) in base)
            known[i, j] = base[a] * base[i - a[0], j - a[1]]
    return [known[e] for e in MOMENTS]


def row_of(n):
    return 16 * (n // 10) + n % 10


def gram_tile(coords, gram, tile, valid, slots):
    zero = jnp.zeros((8, LANES), F32)
    gram[tile, :, 8:16, :] = jnp.zeros((20, 8, LANES), F32)
    gram[tile, :, 24:32, :] = jnp.zeros((20, 8, LANES), F32)

    def sums(terms, which, count):
        def step(i, totals):
            for u in range(UNROLL):
                at = pl.multiple_of((i * UNROLL + u) * 8, 8)
                new = terms(*[coords[c, pl.ds(at, 8), :] for c in which])
                totals = tuple(a + b for a, b in zip(totals, new))
            return totals

        trips = slots // 8 // UNROLL
        totals = step(0, (zero,) * count) if trips == 1 else lax.fori_loop(0, trips, step, (zero,) * count)
        return [jnp.sum(t, axis=0, keepdims=True) for t in totals]

    def put(n, m, row):
        r = row_of(m)
        gram[tile, n, r : r + 1, :] = row

    for side in range(2):
        table = dict(zip(MOMENTS, sums(moments, (2 * side, 2 * side + 1), 27)))
        table[0, 0] = valid
        for n, (i, j) in enumerate(EXPONENTS):
            for m, (k, l) in enumerate(EXPONENTS):
                put(10 * side + n, 10 * side + m, table[i + k, j + l])
        for n, e in enumerate(EXPONENTS):
            if side == 1:
                put(0, 10 + n, table[e])
                put(10 + n, 0, table[e])
            elif n:
                put(10, n, table[e])
                put(n, 10, table[e])
    for some in GROUPS:

        def terms(xa, ya, xb, yb):
            a, b = powers(xa, ya), powers(xb, yb)
            return [a[m] * b[n] for m in some for n in range(1, 10)]

        rows = iter(sums(terms, (0, 1, 2, 3), 9 * len(some)))
        for m in some:
            for n in range(1, 10):
                row = next(rows)
                put(m, 10 + n, row)
                put(10 + n, m, row)


def thirds(x):
    high = x.astype(BF16)
    rest = x - high.astype(F32)
    middle = rest.astype(BF16)
    low = (rest - middle.astype(F32)).astype(BF16)
    return jnp.concatenate([high, middle, low], axis=0)


def joined(x):
    rows = x.shape[0] // 3
    return x[:rows] + x[rows : 2 * rows] + x[2 * rows :]


def matmul(a, b):
    return lax.dot_general(a, b, (((1,), (0,)), ((), ())), preferred_element_type=F32)


def matmul_t(a, b):
    return lax.dot_general(a, b, (((1,), (1,)), ((), ())), preferred_element_type=F32)


def kernel(
    sizes, params_hbm, side_hbm, prior_hbm, matches_hbm, first_hbm, second_hbm, count_hbm, lists_hbm,
    solution_ref, residual_ref,
    first_ref, second_ref, count_ref, lists_ref, params, side, prior, points, coords, sort_ref, gram, own_hot, other_hot, z_ref,
    y_ref, direction, lists_in, halo_in, fold_out, fold_in, part, part_in,
    load_sem, small_sem, field_sem, list_send, list_recv, halo_send, halo_recv, fold_send, fold_recv, part_send, part_recv,
):
    secs, regs, group = sizes
    sec, reg = lax.axis_index("sec"), lax.axis_index("reg")
    pairs = first_hbm.shape[1]
    slots = matches_hbm.shape[2]
    chunks = pairs // LANES
    rows = secs // group

    loads = []
    for i in range(chunks):
        loads.append(pltpu.make_async_copy(matches_hbm.at[pl.ds(i * LANES, LANES)], points.at[i], load_sem.at[i]))
    fields = [
        pltpu.make_async_copy(source.at[:, :, 0, :], target.at[:, pl.ds(0, 10), :], field_sem.at[i])
        for i, (source, target) in enumerate(((params_hbm, params), (side_hbm, side), (prior_hbm, prior)))
    ]
    for target in (params, side, prior):
        target[:, 10:16, :] = jnp.zeros((2, 6, TILES), F32)
    small = [
        pltpu.make_async_copy(source, target, small_sem.at[i])
        for i, (source, target) in enumerate(
            ((lists_hbm, lists_ref), (count_hbm, count_ref), (first_hbm, first_ref), (second_hbm, second_ref))
        )
    ]
    for copy in loads[:1] + small[:1] + fields[:1] + small[1:2] + loads[1:] + small[2:] + fields[1:]:
        copy.start()

    def device(by_sec, by_reg):
        return (lax.rem(sec + by_sec + secs, secs), lax.rem(reg + by_reg + regs, regs))

    borrowers = [device(1, 0), device(2, 0), device(0, 1), device(0, -1)]
    owners = [device(-1, 0), device(-2, 0), device(0, -1), device(0, 1)]
    base, place = group * (sec // group), lax.rem(sec, group)
    line = [(base + lax.rem(place + j, group), reg) for j in sorted(range(1, group), key=lambda j: abs(2 * j - group))]
    hops = [(min(a, rows - a) + min(b, regs - b), a, b) for a in range(rows) for b in range(regs) if a or b]
    plane = [
        (lax.rem(sec // group + a, rows) * group + place, lax.rem(reg + b, regs)) for _, a, b in sorted(hops, reverse=True)
    ]

    halo_in[...] = jnp.zeros_like(halo_in)
    fold_in[...] = jnp.zeros_like(fold_in)
    lists_in[...] = jnp.zeros_like(lists_in)
    barrier = pltpu.get_barrier_semaphore()
    for peer in borrowers + owners[:2] + line + plane:
        pl.semaphore_signal(barrier, inc=1, device_id=peer, device_id_type=MESH)

    above = [sec < secs - 1, sec < secs - 2, reg < regs - 1, reg > 0]
    below = [sec > 0, sec > 1, reg > 0, reg < regs - 1]
    sent = []

    def send(source, target, send_sem, recv_sem, peer, sends=None, receives=None):
        copy = pltpu.make_async_remote_copy(
            src_ref=source, dst_ref=target, send_sem=send_sem, recv_sem=recv_sem, device_id=peer, device_id_type=MESH
        )
        if sends is None:
            copy.start()
            sent.append(copy.wait_send)
            return copy.wait_recv
        pl.when(sends)(copy.start)
        sent.append(lambda: pl.when(sends)(copy.wait_send))
        return lambda: pl.when(receives)(copy.wait_recv)

    def send_halo(source, turn):
        return [
            send(
                source.at[:, pl.ds(0, 10), :], halo_in.at[turn, i, :, pl.ds(0, 10), :], halo_send.at[turn, i], halo_recv.at[turn, i], borrowers[i], above[i], below[i]
            )
            for i in range(4)
        ]

    def send_fold(turn):
        return [
            send(
                fold_out.at[turn, i, :, pl.ds(0, 10), :], fold_in.at[turn, i, :, pl.ds(0, 10), :], fold_send.at[turn, i], fold_recv.at[turn, i], owners[i],
                below[i], above[i],
            )
            for i in range(4)
        ]

    r = lax.broadcasted_iota(jnp.int32, (4 * LANES, 4 * LANES), 0)
    s = lax.broadcasted_iota(jnp.int32, (4 * LANES, 4 * LANES), 1)
    sort_ref[...] = jnp.where(r == 4 * lax.rem(s, LANES) + s // LANES, 1.0, 0.0).astype(BF16)
    slot = lax.broadcasted_iota(jnp.int32, (slots, LANES), 0)

    def turn(tile, to):
        turned = lax.dot_general(
            points[tile].reshape(4 * LANES, slots), sort_ref[...], (((0,), (0,)), ((), ())), preferred_element_type=F32
        )
        live = slot < count_ref[tile]
        for c in range(4):
            coords[to, c] = jnp.where(live, turned[:, c * LANES : (c + 1) * LANES], 0.0)
        coords[to, 4] = jnp.where(live, 1.0, 0.0)

    def gram_of(tile, at):
        gram_tile(coords.at[at], gram, tile, count_ref[tile].astype(F32), slots)

    def form(tile):
        at = lax.rem(tile, 3)
        turn(tile, at)
        gram_of(tile, at)

    for copy in small[1:2] + loads[:1]:
        copy.wait()
    pl.loop(0, EARLY)(form)
    for copy in loads[1:] + small[2:] + fields[1:]:
        copy.wait()
    for copy in fields[:1] + small[:1]:
        copy.wait()
    pl.semaphore_wait(barrier, 6 + len(line) + len(plane))
    halo = send_halo(params, 0)
    borders = [
        send(lists_ref, lists_in.at[0], list_send.at[0], list_recv.at[0], borrowers[2], above[2], below[2]),
        send(lists_ref, lists_in.at[1], list_send.at[1], list_recv.at[1], borrowers[3], above[3], below[3]),
    ]


    pl.loop(EARLY, FORMED)(form)
    for tile in range(FORMED, chunks):
        turn(tile, tile % 3)

    for arrived in borders:
        arrived()
    second = second_ref[...]
    width = lists_ref.shape[1]
    index = jnp.where(second < 3 * TILES, second, -1).astype(F32)
    for i in range(2):
        start = 3 * TILES + i * width
        spot = lax.broadcasted_iota(jnp.int32, (width, pairs), 0) + start
        named = jnp.where(spot == second, 1.0, 0.0).astype(BF16)
        tile_at = matmul((lists_in[i] + 1).astype(F32).astype(BF16), named)[1 - i : 2 - i]
        index = jnp.where(tile_at > 0, tile_at + float((3 + i) * TILES - 1), index)
    index = index.astype(jnp.int32)
    column = lax.broadcasted_iota(jnp.int32, (TILES, pairs), 0)
    own_hot[...] = jnp.where(column == first_ref[...], 1.0, 0.0).astype(BF16)
    for i in range(5):
        other_hot[i * TILES : (i + 1) * TILES, :] = jnp.where(column == index - i * TILES, -1.0, 0.0).astype(BF16)

    def gathered(field, turn, halo):
        mine = thirds(field)
        own = joined(matmul(mine, own_hot[...]))
        other = matmul(mine, other_hot[:TILES, :])
        for arrived in halo:
            arrived()
        others = jnp.concatenate([thirds(halo_in[turn, i].reshape(FIELD, TILES)) for i in range(4)], axis=1)
        other = joined(other + matmul(others, other_hot[TILES:, :]))
        z_ref[0] = own
        z_ref[1] = other

    scale = 2.0 / slots

    def products(tiles):
        for tile in range(tiles):
            at = slice(tile * LANES, (tile + 1) * LANES)
            totals = [None, None]
            for n in range(20):
                block = gram[tile, n]
                for c in range(2):
                    row = 16 * c + n % 10
                    term = block * z_ref[n // 10, row : row + 1, at]
                    totals[c] = term if totals[c] is None else totals[c] + term
            for c in range(2):
                for half in range(2):
                    y_ref[half, 16 * c : 16 * c + 16, at] = totals[c][16 * half : 16 * half + 16]

    def direct(tile):
        at = slice(tile * LANES, (tile + 1) * LANES)
        points_of = coords.at[tile % 3]
        for c in range(2):
            z = [[z_ref[half, 16 * c + m : 16 * c + m + 1, at] for m in range(10)] for half in range(2)]
            constant = z[0][0] + z[1][0]

            def step(i, totals):
                for u in range(UNROLL):
                    here = pl.multiple_of((i * UNROLL + u) * 8, 8)
                    xa, ya, xb, yb, live = [points_of[d, pl.ds(here, 8), :] for d in range(5)]
                    basis = powers(xa, ya)[1:] + powers(xb, yb)[1:]
                    first_half, second_half = constant + z[0][1] * xa, z[1][1] * xb
                    for m in range(1, 9):
                        first_half = first_half + z[0][m + 1] * basis[m]
                        second_half = second_half + z[1][m + 1] * basis[9 + m]
                    mismatch = (first_half + second_half) * live
                    totals = (totals[0] + mismatch,) + tuple(t + b * mismatch for t, b in zip(totals[1:], basis))
                return totals

            totals = lax.fori_loop(0, slots // 8 // UNROLL, step, (jnp.zeros((8, LANES), F32),) * 19)
            totals = [jnp.sum(t, axis=0, keepdims=True) for t in totals]
            for half in range(2):
                y_ref[half, 16 * c : 16 * c + 1, at] = totals[0]
                for m in range(1, 10):
                    y_ref[half, 16 * c + m : 16 * c + m + 1, at] = totals[9 * half + m]

    def scattered(turn):
        own, other = y_ref[0] * scale, y_ref[1] * scale
        others = thirds(other)
        lent = joined(matmul_t(others, other_hot[TILES:, :]))
        for i in range(4):
            fold_out[turn, i] = lent[:, i * TILES : (i + 1) * TILES].reshape(2, FIELD // 2, TILES)
        fold = send_fold(turn)
        local = joined(matmul_t(thirds(own), own_hot[...]) + matmul_t(others, other_hot[:TILES, :]))
        return fold, local

    def folded(fold, local, turn):
        for arrived in fold:
            arrived()
        return local + jnp.sum(fold_in[turn], axis=0).reshape(FIELD, TILES)

    start = params[...].reshape(FIELD, TILES)
    gathered(start, 0, halo)
    for c in range(2):
        for half in range(2):
            y_ref[half, 16 * c + 10 : 16 * c + 16, :] = jnp.zeros((6, pairs), F32)
    for tile in range(FORMED, chunks):
        direct(tile)
    products(FORMED)
    fold, local = scattered(0)
    for tile in range(FORMED, chunks - 2):
        gram_of(tile, tile % 3)
    local = local + prior[...].reshape(FIELD, TILES) * start
    residual = side[...].reshape(FIELD, TILES) - folded(fold, local, 0)

    direction[...] = residual.reshape(2, FIELD // 2, TILES)
    halo = send_halo(direction, 1)
    gram_of(chunks - 2, (chunks - 2) % 3)
    gram_of(chunks - 1, (chunks - 1) % 3)
    squares = jnp.sum(residual * residual, keepdims=True)
    damped = prior[...].reshape(FIELD, TILES) * residual
    gathered(residual, 1, halo)
    products(chunks)
    energy = scale * jnp.sum(y_ref[0] * z_ref[0] + y_ref[1] * z_ref[1], keepdims=True) + jnp.sum(damped * residual, keepdims=True)
    lane = lax.broadcasted_iota(jnp.int32, (1, LANES), 1)
    total = jnp.where(lane < LANES // 2, squares, energy)
    part[0, 0:1, :] = total

    def send_part(turn, peers):
        return [
            send(
                part.at[turn, pl.ds(0, 1), :], part_in.at[turn, pl.ds(j, 1), :],
                part_send.at[turn, j], part_recv.at[turn, j], peer,
            )
            for j, peer in enumerate(peers)
        ]

    sums = send_part(0, line)
    fold, local = scattered(1)
    local = local + damped
    for arrived in sums:
        arrived()
    total = total + jnp.sum(part_in[0, : len(line), :], axis=0, keepdims=True)
    part[1, 0:1, :] = total
    sums = send_part(1, plane)
    image = folded(fold, local, 1)
    for left_here in sent:
        left_here()
    for arrived in sums:
        arrived()
    total = total + jnp.sum(part_in[1, : len(plane), :], axis=0, keepdims=True)
    alpha = total[:, 0:1] / total[:, LANES // 2 : LANES // 2 + 1]
    answer = start + alpha * residual
    left = residual - alpha * image
    for c in range(2):
        for value, target in ((answer, solution_ref), (left, residual_ref)):
            target[10 * c : 10 * c + 10, :] = value[16 * c : 16 * c + 10]


def on_device(sizes, start_params, right_side, prior, matches, pair_first, pair_second, match_counts, send_lists):
    pairs, slots = matches.shape[2], matches.shape[4]
    width = send_lists.shape[3]
    secs, regs, group = sizes
    part_rows = -(-max(group, secs // group * regs) // 8) * 8
    chunks = pairs // LANES
    vmem = pl.BlockSpec(memory_space=pltpu.VMEM)
    hbm = pl.BlockSpec(memory_space=pltpu.HBM)
    field, split = (FIELD, TILES), (2, FIELD // 2, TILES)
    dma = pltpu.SemaphoreType.DMA
    answer, left = pl.pallas_call(
        functools.partial(kernel, sizes),
        out_shape=(jax.ShapeDtypeStruct((20, TILES), F32),) * 2,
        in_specs=[hbm] * 8,
        out_specs=(vmem, vmem),
        scratch_shapes=[
            pltpu.VMEM((1, pairs), jnp.int32),
            pltpu.VMEM((1, pairs), jnp.int32),
            pltpu.VMEM((chunks, 1, LANES), jnp.int32),
            pltpu.VMEM((2, width), jnp.int32),
            pltpu.VMEM(split, F32),
            pltpu.VMEM(split, F32),
            pltpu.VMEM(split, F32),
            pltpu.VMEM((chunks, LANES, 4, slots), BF16),
            pltpu.VMEM((3, 5, slots, LANES), F32),
            pltpu.VMEM((4 * LANES, 4 * LANES), BF16),
            pltpu.VMEM((chunks, 20, FIELD, LANES), F32),
            pltpu.VMEM((TILES, pairs), BF16),
            pltpu.VMEM((5 * TILES, pairs), BF16),
            pltpu.VMEM((2, FIELD, pairs), F32),
            pltpu.VMEM((2, FIELD, pairs), F32),
            pltpu.VMEM(split, F32),
            pltpu.VMEM((2, 2, width), jnp.int32),
            pltpu.VMEM((2, 4, *split), F32),
            pltpu.VMEM((2, 4, *split), F32),
            pltpu.VMEM((2, 4, *split), F32),
            pltpu.VMEM((2, 8, LANES), F32),
            pltpu.VMEM((2, part_rows, LANES), F32),
            dma((chunks,)),
            dma((4,)),
            dma((3,)),
            dma((2,)),
            dma((2,)),
            dma((2, 4)),
            dma((2, 4)),
            dma((2, 4)),
            dma((2, 4)),
            dma((2, part_rows)),
            dma((2, part_rows)),
        ],
        compiler_params=pltpu.CompilerParams(collective_id=0, has_side_effects=True, vmem_limit_bytes=32 * 2**20),
    )(*[pltpu.with_memory_space_constraint(x, pltpu.HBM) for x in (
        start_params.reshape(2, 10, 1, TILES),
        right_side.reshape(2, 10, 1, TILES),
        prior.reshape(2, 10, 1, TILES),
        matches.reshape(pairs, 4, slots),
        pair_first.reshape(1, pairs),
        pair_second.reshape(1, pairs),
        match_counts.reshape(chunks, 1, LANES),
        send_lists.reshape(2, width),
    )])
    return answer[None, None], left[None, None]


def solution(mesh):
    secs, regs = mesh.shape["sec"], mesh.shape["reg"]
    group = 16 if secs % 16 == 0 else secs
    wide = P("sec", "reg", None, None)
    return jax.shard_map(
        functools.partial(on_device, (secs, regs, group)),
        mesh=mesh,
        in_specs=(
            wide, wide, wide, P("sec", "reg", None, None, None),
            P("sec", "reg", None), P("sec", "reg", None), P("sec", "reg", None), wide,
        ),
        out_specs=(wide, wide),
        check_vma=False,
    )
```

```python
import functools

import jax
import jax.numpy as jnp
from jax import lax
from jax.experimental import pallas as pl
from jax.experimental.pallas import tpu as pltpu
from jax.sharding import PartitionSpec as P

F32, BF16 = jnp.float32, jnp.bfloat16
MESH = pl.DeviceIdType.MESH
EXPONENTS = [(0, 0), (1, 0), (0, 1), (2, 0), (1, 1), (0, 2), (3, 0), (2, 1), (1, 2), (0, 3)]
MOMENTS = [(i, d - i) for d in range(1, 7) for i in range(d, -1, -1)]
TILES = 128
LANES = 128
FIELD = 32
UNROLL = 16
EARLY = 1
FORMED = 2
GROUPS = ((1, 2, 3), (4, 5, 6), (7, 8, 9))


def powers(x, y):
    x2, xy, y2 = x * x, x * y, y * y
    return [None, x, y, x2, xy, y2, x2 * x, x2 * y, y2 * x, y2 * y]


def moments(x, y):
    base = dict(zip(EXPONENTS, powers(x, y)))
    known = dict(base)
    for i, j in MOMENTS:
        if (i, j) not in known:
            a = next(e for e in EXPONENTS[:2:-1] if (i - e[0], j - e[1]) in base)
            known[i, j] = base[a] * base[i - a[0], j - a[1]]
    return [known[e] for e in MOMENTS]


def row_of(n):
    return 16 * (n // 10) + n % 10


def gram_tile(coords, gram, tile, valid, slots):
    zero = jnp.zeros((8, LANES), F32)
    gram[tile, :, 8:16, :] = jnp.zeros((20, 8, LANES), F32)
    gram[tile, :, 24:32, :] = jnp.zeros((20, 8, LANES), F32)

    def sums(terms, which, count):
        def step(i, totals):
            for u in range(UNROLL):
                at = pl.multiple_of((i * UNROLL + u) * 8, 8)
                new = terms(*[coords[c, pl.ds(at, 8), :] for c in which])
                totals = tuple(a + b for a, b in zip(totals, new))
            return totals

        trips = slots // 8 // UNROLL
        totals = step(0, (zero,) * count) if trips == 1 else lax.fori_loop(0, trips, step, (zero,) * count)
        return [jnp.sum(t, axis=0, keepdims=True) for t in totals]

    def put(n, m, row):
        r = row_of(m)
        gram[tile, n, r : r + 1, :] = row

    for side in range(2):
        table = dict(zip(MOMENTS, sums(moments, (2 * side, 2 * side + 1), 27)))
        table[0, 0] = valid
        for n, (i, j) in enumerate(EXPONENTS):
            for m, (k, l) in enumerate(EXPONENTS):
                put(10 * side + n, 10 * side + m, table[i + k, j + l])
        for n, e in enumerate(EXPONENTS):
            if side == 1:
                put(0, 10 + n, table[e])
                put(10 + n, 0, table[e])
            elif n:
                put(10, n, table[e])
                put(n, 10, table[e])
    for some in GROUPS:

        def terms(xa, ya, xb, yb):
            a, b = powers(xa, ya), powers(xb, yb)
            return [a[m] * b[n] for m in some for n in range(1, 10)]

        rows = iter(sums(terms, (0, 1, 2, 3), 9 * len(some)))
        for m in some:
            for n in range(1, 10):
                row = next(rows)
                put(m, 10 + n, row)
                put(10 + n, m, row)


def thirds(x):
    high = x.astype(BF16)
    rest = x - high.astype(F32)
    middle = rest.astype(BF16)
    low = (rest - middle.astype(F32)).astype(BF16)
    return jnp.concatenate([high, middle, low], axis=0)


def joined(x):
    rows = x.shape[0] // 3
    return x[:rows] + x[rows : 2 * rows] + x[2 * rows :]


def matmul(a, b):
    return lax.dot_general(a, b, (((1,), (0,)), ((), ())), preferred_element_type=F32)


def matmul_t(a, b):
    return lax.dot_general(a, b, (((1,), (1,)), ((), ())), preferred_element_type=F32)


def kernel(
    sizes, params_hbm, side_hbm, prior_hbm, matches_hbm, first_hbm, second_hbm, count_hbm, lists_hbm,
    solution_ref, residual_ref,
    first_ref, second_ref, count_ref, lists_ref, params, side, prior, points, coords, sort_ref, gram, own_hot, other_hot, z_ref,
    y_ref, direction, lists_in, halo_in, fold_out, fold_in, part, part_in,
    load_sem, small_sem, field_sem, list_send, list_recv, halo_send, halo_recv, fold_send, fold_recv, part_send, part_recv,
):
    secs, regs, group = sizes
    sec, reg = lax.axis_index("sec"), lax.axis_index("reg")
    pairs = first_hbm.shape[1]
    slots = matches_hbm.shape[2]
    chunks = pairs // LANES
    rows = secs // group

    loads = []
    for i in range(chunks):
        loads.append(pltpu.make_async_copy(matches_hbm.at[pl.ds(i * LANES, LANES)], points.at[i], load_sem.at[i]))
    fields = [
        pltpu.make_async_copy(source.at[:, :, 0, :], target.at[:, pl.ds(0, 10), :], field_sem.at[i])
        for i, (source, target) in enumerate(((params_hbm, params), (side_hbm, side), (prior_hbm, prior)))
    ]
    for target in (params, side, prior):
        target[:, 10:16, :] = jnp.zeros((2, 6, TILES), F32)
    small = [
        pltpu.make_async_copy(source, target, small_sem.at[i])
        for i, (source, target) in enumerate(
            ((lists_hbm, lists_ref), (count_hbm, count_ref), (first_hbm, first_ref), (second_hbm, second_ref))
        )
    ]
    for copy in loads[:1] + small[:1] + fields[:1] + small[1:2] + loads[1:] + small[2:] + fields[1:]:
        copy.start()

    def device(by_sec, by_reg):
        return (lax.rem(sec + by_sec + secs, secs), lax.rem(reg + by_reg + regs, regs))

    borrowers = [device(1, 0), device(2, 0), device(0, 1), device(0, -1)]
    owners = [device(-1, 0), device(-2, 0), device(0, -1), device(0, 1)]
    base, place = group * (sec // group), lax.rem(sec, group)
    line = [(base + lax.rem(place + j, group), reg) for j in sorted(range(1, group), key=lambda j: abs(2 * j - group))]
    hops = [(min(a, rows - a) + min(b, regs - b), a, b) for a in range(rows) for b in range(regs) if a or b]
    plane = [
        (lax.rem(sec // group + a, rows) * group + place, lax.rem(reg + b, regs)) for _, a, b in sorted(hops, reverse=True)
    ]

    halo_in[...] = jnp.zeros_like(halo_in)
    fold_in[...] = jnp.zeros_like(fold_in)
    lists_in[...] = jnp.zeros_like(lists_in)
    barrier = pltpu.get_barrier_semaphore()
    for peer in [p for both in zip(line, plane) for p in both] + line[len(plane) :] + plane[len(line) :] + borrowers + owners[:2]:
        pl.semaphore_signal(barrier, inc=1, device_id=peer, device_id_type=MESH)

    above = [sec < secs - 1, sec < secs - 2, reg < regs - 1, reg > 0]
    below = [sec > 0, sec > 1, reg > 0, reg < regs - 1]
    sent = []

    def send(source, target, send_sem, recv_sem, peer, sends=None, receives=None):
        copy = pltpu.make_async_remote_copy(
            src_ref=source, dst_ref=target, send_sem=send_sem, recv_sem=recv_sem, device_id=peer, device_id_type=MESH
        )
        if sends is None:
            copy.start()
            sent.append(copy.wait_send)
            return copy.wait_recv
        pl.when(sends)(copy.start)
        sent.append(lambda: pl.when(sends)(copy.wait_send))
        return lambda: pl.when(receives)(copy.wait_recv)

    def send_halo(source, turn):
        return [
            send(
                source.at[:, pl.ds(0, 10), :], halo_in.at[turn, i, :, pl.ds(0, 10), :], halo_send.at[turn, i], halo_recv.at[turn, i], borrowers[i], above[i], below[i]
            )
            for i in range(4)
        ]

    def send_fold(turn):
        return [
            send(
                fold_out.at[turn, i, :, pl.ds(0, 10), :], fold_in.at[turn, i, :, pl.ds(0, 10), :], fold_send.at[turn, i], fold_recv.at[turn, i], owners[i],
                below[i], above[i],
            )
            for i in range(4)
        ]

    r = lax.broadcasted_iota(jnp.int32, (4 * LANES, 4 * LANES), 0)
    s = lax.broadcasted_iota(jnp.int32, (4 * LANES, 4 * LANES), 1)
    sort_ref[...] = jnp.where(r == 4 * lax.rem(s, LANES) + s // LANES, 1.0, 0.0).astype(BF16)
    slot = lax.broadcasted_iota(jnp.int32, (slots, LANES), 0)

    def turn(tile, to):
        turned = lax.dot_general(
            points[tile].reshape(4 * LANES, slots), sort_ref[...], (((0,), (0,)), ((), ())), preferred_element_type=F32
        )
        live = slot < count_ref[tile]
        for c in range(4):
            coords[to, c] = jnp.where(live, turned[:, c * LANES : (c + 1) * LANES], 0.0)
        coords[to, 4] = jnp.where(live, 1.0, 0.0)

    def gram_of(tile, at):
        gram_tile(coords.at[at], gram, tile, count_ref[tile].astype(F32), slots)

    def form(tile):
        at = lax.rem(tile, 3)
        turn(tile, at)
        gram_of(tile, at)

    for copy in small[1:2] + loads[:1]:
        copy.wait()
    pl.loop(0, EARLY)(form)
    for copy in loads[1:] + small[2:] + fields[1:]:
        copy.wait()
    for copy in fields[:1] + small[:1]:
        copy.wait()
    pl.semaphore_wait(barrier, 6 + len(line) + len(plane))
    halo = send_halo(params, 0)
    borders = [
        send(lists_ref, lists_in.at[0], list_send.at[0], list_recv.at[0], borrowers[2], above[2], below[2]),
        send(lists_ref, lists_in.at[1], list_send.at[1], list_recv.at[1], borrowers[3], above[3], below[3]),
    ]


    pl.loop(EARLY, FORMED)(form)
    for tile in range(FORMED, chunks):
        turn(tile, tile % 3)

    for arrived in borders:
        arrived()
    second = second_ref[...]
    width = lists_ref.shape[1]
    index = jnp.where(second < 3 * TILES, second, -1).astype(F32)
    for i in range(2):
        start = 3 * TILES + i * width
        spot = lax.broadcasted_iota(jnp.int32, (width, pairs), 0) + start
        named = jnp.where(spot == second, 1.0, 0.0).astype(BF16)
        tile_at = matmul((lists_in[i] + 1).astype(F32).astype(BF16), named)[1 - i : 2 - i]
        index = jnp.where(tile_at > 0, tile_at + float((3 + i) * TILES - 1), index)
    index = index.astype(jnp.int32)
    column = lax.broadcasted_iota(jnp.int32, (TILES, pairs), 0)
    own_hot[...] = jnp.where(column == first_ref[...], 1.0, 0.0).astype(BF16)
    for i in range(5):
        other_hot[i * TILES : (i + 1) * TILES, :] = jnp.where(column == index - i * TILES, -1.0, 0.0).astype(BF16)

    def gathered(field, turn, halo):
        mine = thirds(field)
        own = joined(matmul(mine, own_hot[...]))
        other = matmul(mine, other_hot[:TILES, :])
        for arrived in halo:
            arrived()
        others = jnp.concatenate([thirds(halo_in[turn, i].reshape(FIELD, TILES)) for i in range(4)], axis=1)
        other = joined(other + matmul(others, other_hot[TILES:, :]))
        z_ref[0] = own
        z_ref[1] = other

    scale = 2.0 / slots

    def products(tiles):
        for tile in range(tiles):
            at = slice(tile * LANES, (tile + 1) * LANES)
            totals = [None, None]
            for n in range(20):
                block = gram[tile, n]
                for c in range(2):
                    row = 16 * c + n % 10
                    term = block * z_ref[n // 10, row : row + 1, at]
                    totals[c] = term if totals[c] is None else totals[c] + term
            for c in range(2):
                for half in range(2):
                    y_ref[half, 16 * c : 16 * c + 16, at] = totals[c][16 * half : 16 * half + 16]

    def direct(tile):
        at = slice(tile * LANES, (tile + 1) * LANES)
        points_of = coords.at[tile % 3]
        for c in range(2):
            z = [[z_ref[half, 16 * c + m : 16 * c + m + 1, at] for m in range(10)] for half in range(2)]
            constant = z[0][0] + z[1][0]

            def step(i, totals):
                for u in range(UNROLL):
                    here = pl.multiple_of((i * UNROLL + u) * 8, 8)
                    xa, ya, xb, yb, live = [points_of[d, pl.ds(here, 8), :] for d in range(5)]
                    basis = powers(xa, ya)[1:] + powers(xb, yb)[1:]
                    first_half, second_half = constant + z[0][1] * xa, z[1][1] * xb
                    for m in range(1, 9):
                        first_half = first_half + z[0][m + 1] * basis[m]
                        second_half = second_half + z[1][m + 1] * basis[9 + m]
                    mismatch = (first_half + second_half) * live
                    totals = (totals[0] + mismatch,) + tuple(t + b * mismatch for t, b in zip(totals[1:], basis))
                return totals

            totals = lax.fori_loop(0, slots // 8 // UNROLL, step, (jnp.zeros((8, LANES), F32),) * 19)
            totals = [jnp.sum(t, axis=0, keepdims=True) for t in totals]
            for half in range(2):
                y_ref[half, 16 * c : 16 * c + 1, at] = totals[0]
                for m in range(1, 10):
                    y_ref[half, 16 * c + m : 16 * c + m + 1, at] = totals[9 * half + m]

    def scattered(turn):
        own, other = y_ref[0] * scale, y_ref[1] * scale
        others = thirds(other)
        lent = joined(matmul_t(others, other_hot[TILES:, :]))
        for i in range(4):
            fold_out[turn, i] = lent[:, i * TILES : (i + 1) * TILES].reshape(2, FIELD // 2, TILES)
        fold = send_fold(turn)
        local = joined(matmul_t(thirds(own), own_hot[...]) + matmul_t(others, other_hot[:TILES, :]))
        return fold, local

    def folded(fold, local, turn):
        for arrived in fold:
            arrived()
        return local + jnp.sum(fold_in[turn], axis=0).reshape(FIELD, TILES)

    start = params[...].reshape(FIELD, TILES)
    gathered(start, 0, halo)
    for c in range(2):
        for half in range(2):
            y_ref[half, 16 * c + 10 : 16 * c + 16, :] = jnp.zeros((6, pairs), F32)
    for tile in range(FORMED, chunks):
        direct(tile)
    products(FORMED)
    fold, local = scattered(0)
    for tile in range(FORMED, chunks - 2):
        gram_of(tile, tile % 3)
    local = local + prior[...].reshape(FIELD, TILES) * start
    residual = side[...].reshape(FIELD, TILES) - folded(fold, local, 0)

    direction[...] = residual.reshape(2, FIELD // 2, TILES)
    halo = send_halo(direction, 1)
    gram_of(chunks - 2, (chunks - 2) % 3)
    gram_of(chunks - 1, (chunks - 1) % 3)
    squares = jnp.sum(residual * residual, keepdims=True)
    damped = prior[...].reshape(FIELD, TILES) * residual
    gathered(residual, 1, halo)
    products(chunks)
    energy = scale * jnp.sum(y_ref[0] * z_ref[0] + y_ref[1] * z_ref[1], keepdims=True) + jnp.sum(damped * residual, keepdims=True)
    lane = lax.broadcasted_iota(jnp.int32, (1, LANES), 1)
    total = jnp.where(lane < LANES // 2, squares, energy)
    part[0, 0:1, :] = total

    def send_part(turn, peers):
        return [
            send(
                part.at[turn, pl.ds(0, 1), :], part_in.at[turn, pl.ds(j, 1), :],
                part_send.at[turn, j], part_recv.at[turn, j], peer,
            )
            for j, peer in enumerate(peers)
        ]

    sums = send_part(0, line)
    fold, local = scattered(1)
    local = local + damped
    for arrived in sums:
        arrived()
    total = total + jnp.sum(part_in[0, : len(line), :], axis=0, keepdims=True)
    part[1, 0:1, :] = total
    sums = send_part(1, plane)
    image = folded(fold, local, 1)
    for left_here in sent:
        left_here()
    for arrived in sums:
        arrived()
    total = total + jnp.sum(part_in[1, : len(plane), :], axis=0, keepdims=True)
    alpha = total[:, 0:1] / total[:, LANES // 2 : LANES // 2 + 1]
    answer = start + alpha * residual
    left = residual - alpha * image
    for c in range(2):
        for value, target in ((answer, solution_ref), (left, residual_ref)):
            target[10 * c : 10 * c + 10, :] = value[16 * c : 16 * c + 10]


def on_device(sizes, start_params, right_side, prior, matches, pair_first, pair_second, match_counts, send_lists):
    pairs, slots = matches.shape[2], matches.shape[4]
    width = send_lists.shape[3]
    secs, regs, group = sizes
    part_rows = -(-max(group, secs // group * regs) // 8) * 8
    chunks = pairs // LANES
    vmem = pl.BlockSpec(memory_space=pltpu.VMEM)
    hbm = pl.BlockSpec(memory_space=pltpu.HBM)
    field, split = (FIELD, TILES), (2, FIELD // 2, TILES)
    dma = pltpu.SemaphoreType.DMA
    answer, left = pl.pallas_call(
        functools.partial(kernel, sizes),
        out_shape=(jax.ShapeDtypeStruct((20, TILES), F32),) * 2,
        in_specs=[hbm] * 8,
        out_specs=(vmem, vmem),
        scratch_shapes=[
            pltpu.VMEM((1, pairs), jnp.int32),
            pltpu.VMEM((1, pairs), jnp.int32),
            pltpu.VMEM((chunks, 1, LANES), jnp.int32),
            pltpu.VMEM((2, width), jnp.int32),
            pltpu.VMEM(split, F32),
            pltpu.VMEM(split, F32),
            pltpu.VMEM(split, F32),
            pltpu.VMEM((chunks, LANES, 4, slots), BF16),
            pltpu.VMEM((3, 5, slots, LANES), F32),
            pltpu.VMEM((4 * LANES, 4 * LANES), BF16),
            pltpu.VMEM((chunks, 20, FIELD, LANES), F32),
            pltpu.VMEM((TILES, pairs), BF16),
            pltpu.VMEM((5 * TILES, pairs), BF16),
            pltpu.VMEM((2, FIELD, pairs), F32),
            pltpu.VMEM((2, FIELD, pairs), F32),
            pltpu.VMEM(split, F32),
            pltpu.VMEM((2, 2, width), jnp.int32),
            pltpu.VMEM((2, 4, *split), F32),
            pltpu.VMEM((2, 4, *split), F32),
            pltpu.VMEM((2, 4, *split), F32),
            pltpu.VMEM((2, 8, LANES), F32),
            pltpu.VMEM((2, part_rows, LANES), F32),
            dma((chunks,)),
            dma((4,)),
            dma((3,)),
            dma((2,)),
            dma((2,)),
            dma((2, 4)),
            dma((2, 4)),
            dma((2, 4)),
            dma((2, 4)),
            dma((2, part_rows)),
            dma((2, part_rows)),
        ],
        compiler_params=pltpu.CompilerParams(collective_id=0, has_side_effects=True, vmem_limit_bytes=32 * 2**20),
    )(*[pltpu.with_memory_space_constraint(x, pltpu.HBM) for x in (
        start_params.reshape(2, 10, 1, TILES),
        right_side.reshape(2, 10, 1, TILES),
        prior.reshape(2, 10, 1, TILES),
        matches.reshape(pairs, 4, slots),
        pair_first.reshape(1, pairs),
        pair_second.reshape(1, pairs),
        match_counts.reshape(chunks, 1, LANES),
        send_lists.reshape(2, width),
    )])
    return answer[None, None], left[None, None]


def solution(mesh):
    secs, regs = mesh.shape["sec"], mesh.shape["reg"]
    group = 16 if secs % 16 == 0 else secs
    wide = P("sec", "reg", None, None)
    return jax.shard_map(
        functools.partial(on_device, (secs, regs, group)),
        mesh=mesh,
        in_specs=(
            wide, wide, wide, P("sec", "reg", None, None, None),
            P("sec", "reg", None), P("sec", "reg", None), P("sec", "reg", None), wide,
        ),
        out_specs=(wide, wide),
        check_vma=False,
    )
```
